32 devices in a mesh: seq: 8 (over z, x), tp: 4 (over y, core).
Axes of the slice: x: 2, y: 2, z: 4, core: 2. Of those that a mesh axis runs over, the one named last changes fastest.
Arguments:
- queries: bfloat16 [4096, 4096], P('seq', 'tp'), may hold values from -6 to 6
- keys: bfloat16 [4096, 4096], P('seq', 'tp'), may hold values from -6 to 6
- values: bfloat16 [4096, 4096], P('seq', 'tp'), may hold values from -6 to 6
- grad_out: bfloat16 [4096, 4096], P('seq', 'tp'), may hold values from -16 to 16
- out_weight: bfloat16 [4096, 4096], P('tp'), may hold values from -0.09375 to 0.09375
- norm_gain: float32 [4096], P('tp'), may hold values from 0.1 to 1.9
- doc_ids: int32 [4096], P('seq'), may hold values from 0 to 3, never falling along the last dimension, each value on 1 to 2048 neighbouring positions
Outputs:
- query_grad: bfloat16 [4096, 4096], P('seq', 'tp')
- key_grad: bfloat16 [4096, 4096], P('seq', 'tp')
- value_grad: bfloat16 [4096, 4096], P('seq', 'tp')
- out_proj_grad: float32 [4096, 4096], P('seq', 'tp')
The draws below stay inside these ranges and needn't reach their ends.
Inputs may be any that keep to these rules, and one draw needn't show every extreme that they name: `doc_ids`: document ids never fall along the sequence; each document has 1 to 2048 positions and one has exactly 2048.
All inputs are finite; a program needn't handle non-finite values.
Results may differ from the reference program's by a relative error of at most 0.012.
Values may be sent and summed in bfloat16 or wider, within the bound.
A program may use at most 128 MiB of HBM per device.

```python
import math
import jax
import jax.numpy as jnp
import numpy as np
from jax import lax

D = 4096
HEADS = 32
HEAD_DIM = 128
DOCS = 4
BLOCK = 512
TOKENS = 4096


def spiked(values, own_key, source, target, shards_of, factor):
    def block_of(axis_at):
        return (jnp.arange(values.shape[axis_at]) // (values.shape[axis_at] // shards_of)).reshape((-1,) + (1,) * (values.ndim - 1 - axis_at))

    near = jax.random.permutation(own_key, shards_of)[block_of(target)]
    second = (block_of(target) + shards_of // 2) % shards_of
    return jnp.where((block_of(source) == near) | (block_of(source) == second), factor * values, values)


def block_scale(own_key, extent, pieces, low, largest):
    level, own = 1.0, jax.random.fold_in(own_key, 6)
    for axis_at, parts in pieces:
        draws = jnp.exp(jax.random.uniform(jax.random.fold_in(own, axis_at), (parts,), jnp.float32, low / len(pieces), largest / len(pieces)))
        level = level * jnp.repeat(draws, extent[axis_at] // parts).reshape([-1 if axis == axis_at else 1 for axis in range(len(extent))])
    return level


def profile(number_of, total, bound, skew):
    portions = [(1 << 20) // math.isqrt(rank ** skew) + 1 for rank in range(2, number_of + 1)]
    rest, counts = total - bound - (number_of - 1), [1] * (number_of - 1)
    while rest > 0:
        free = [i for i in range(number_of - 1) if counts[i] < bound]
        pool, budget = sum([portions[i] for i in free]), rest
        for i in free:
            more = min(bound - counts[i], max(1, budget * portions[i] // pool), rest)
            counts[i] = counts[i] + more
            rest = rest - more
    return np.array([bound] + counts)


def uneven(rng, count, total, most, skew):
    if count == 2:
        one = jax.random.randint(rng, (), max(1, total - most), min(most, total - 1) + 1)
        return jnp.stack([one, total - one])
    lengths = jnp.asarray(profile(count, total, most, skew), jnp.int32)
    pairs = (count - 1) // 2
    donor, sink = lengths[1:1 + 2 * pairs:2], lengths[2:2 + 2 * pairs:2]
    margin = jnp.minimum(donor - 1, most - sink)
    shifted = jax.random.randint(jax.random.fold_in(rng, 1), (pairs,), 0, 1 << 20) % (margin + 1)
    lengths = lengths.at[1:1 + 2 * pairs:2].set(donor - shifted).at[2:2 + 2 * pairs:2].set(sink + shifted)
    return lengths[jax.random.permutation(jax.random.fold_in(rng, 2), count)]


def centred(rng, dims, scale, most, cuts=(), held_as=jnp.bfloat16):
    loudness = block_scale(rng, dims, cuts, -0.22, 0.18) if cuts else 1.0
    result = jax.random.normal(rng, dims, jnp.float32) * scale * loudness
    return jnp.minimum(jnp.maximum(result, -most), most).astype(held_as)


def gaussian_with(key, dims, deviation, most, shards, heavy, dtype=jnp.bfloat16):
    entries = deviation * jax.random.normal(key, dims, jnp.float32)
    if shards:
        entries = entries * block_scale(key, dims, shards, -0.22, 0.18)
    return jnp.clip(spiked(entries, jax.random.fold_in(key, 3), *heavy), -most, most).astype(dtype)


def setup_inputs(seed: int = 0) -> dict:
    splits = jax.random.split(jax.random.key(seed), 8)
    queries = centred(splits[0], (TOKENS, HEADS * HEAD_DIM), 1.0, 6.0, ((0, 8), (1, 4)))
    keys = centred(splits[1], (TOKENS, HEADS * HEAD_DIM), 1.0, 6.0, ((0, 8), (1, 4)))
    values = centred(splits[2], (TOKENS, HEADS * HEAD_DIM), 1.0, 6.0, ((0, 8), (1, 4)))
    grad_out = gaussian_with(splits[3], (TOKENS, D), 4.0, 16.0, ((0, 8), (1, 4)), (0, 1, 8, 2.0))
    out_weight = centred(splits[4], (HEADS * HEAD_DIM, D), (HEADS * HEAD_DIM) ** -0.5, 0.09375, ((0, 4),))
    norm_gain = jnp.clip(1.0 + 0.18 * jax.random.normal(splits[5], (HEADS * HEAD_DIM,), jnp.float32), 0.1, 1.9)
    doc_ids = jnp.searchsorted(jnp.cumsum(uneven(splits[6], DOCS, TOKENS, TOKENS // 2, 2)), jnp.arange(TOKENS), side="right").astype(jnp.int32)
    return {"queries": queries, "keys": keys, "values": values, "grad_out": grad_out, "out_weight": out_weight, "norm_gain": norm_gain, "doc_ids": doc_ids}


EPS = 1e-06

def feature(x):
    return jnp.where(x > 0, x + 1.0, jnp.exp(jnp.minimum(x, 0.0)))

def feature_slope(x):
    return jnp.where(x > 0, 1.0, jnp.exp(jnp.minimum(x, 0.0)))

def combine(earlier, later):
    state_early, tag_early = earlier
    state_late, tag_late = later
    vacant = tag_late < 0
    joined = state_late + jnp.where(tag_early == tag_late, state_early, 0.0)
    return (jnp.where(vacant, state_early, joined), jnp.where(vacant, tag_early, tag_late))

def reference(queries, keys, values, grad_out, out_weight, norm_gain, doc_ids):
    block_count = TOKENS // BLOCK
    feat_q = feature(queries.astype(jnp.float32)).astype(jnp.bfloat16)
    feat_k = feature(keys.astype(jnp.float32)).astype(jnp.bfloat16)

    def split(array):
        return array.reshape(block_count, BLOCK, HEADS, HEAD_DIM)
    doc_float = doc_ids.astype(jnp.float32).reshape(block_count, BLOCK)
    positions = jnp.arange(BLOCK)
    causal = positions[:, None] >= positions[None, :]
    gain = norm_gain.astype(jnp.float32).reshape(HEADS, HEAD_DIM)

    def pair_weights(query_block, key_block, doc_block):
        allowed = causal & (doc_block[:, None] == doc_block[None, :])
        scores = jnp.einsum('thd,shd->hts', query_block.astype(jnp.float32), key_block.astype(jnp.float32))
        return (jnp.where(allowed[None], scores, 0.0).astype(jnp.bfloat16), allowed)
    start_state = (jnp.zeros((HEADS, HEAD_DIM, HEAD_DIM), jnp.float32), jnp.array(-1.0, jnp.float32))

    def forward_step(carry, items):
        query_block, key_block, value_block, doc_block = items
        state, tag = carry
        weight, allowed = pair_weights(query_block, key_block, doc_block)
        inner = jnp.einsum('hts,she->the', weight.astype(jnp.float32), value_block.astype(jnp.float32))
        rounded = state.astype(jnp.bfloat16).astype(jnp.float32)
        outer = jnp.einsum('thd,hde->the', query_block.astype(jnp.float32), rounded)
        attn = inner + jnp.where((doc_block == tag)[:, None, None], outer, 0.0)
        last_doc = doc_block[-1]
        chosen = (doc_block == last_doc)[:, None, None]
        summary = jnp.einsum('shd,she->hde', jnp.where(chosen, key_block.astype(jnp.float32), 0.0), value_block.astype(jnp.float32))
        return (combine(carry, (summary, last_doc)), (attn, state, tag))
    _, (attn, states, tags) = lax.scan(forward_step, start_state, (split(feat_q), split(feat_k), split(values), doc_float))
    inv_rms = lax.rsqrt(lax.optimization_barrier(jnp.mean(attn * attn, axis=-1, keepdims=True)) + EPS)
    normed = (attn * inv_rms * gain).astype(jnp.bfloat16)
    upstream = jnp.dot(grad_out, out_weight.T, preferred_element_type=jnp.float32)
    scaled = split(upstream) * gain
    grad_attn = (scaled * inv_rms - attn * inv_rms ** 3 * lax.optimization_barrier(jnp.mean(attn * scaled, axis=-1, keepdims=True))).astype(jnp.bfloat16)
    out_proj_grad = jnp.dot(grad_out.T, normed.reshape(TOKENS, HEADS * HEAD_DIM), preferred_element_type=jnp.float32) * (1.0 / math.sqrt(TOKENS))

    def backward_step(carry, items):
        query_block, key_block, value_block, doc_block, grad_block, state, tag, raw_query, raw_key = items
        dstate, dtag = carry
        weight, allowed = pair_weights(query_block, key_block, doc_block)
        qf = query_block.astype(jnp.float32)
        kf = key_block.astype(jnp.float32)
        vf = value_block.astype(jnp.float32)
        gf = grad_block.astype(jnp.float32)
        grad_weight = jnp.where(allowed[None], jnp.einsum('the,she->hts', gf, vf), 0.0).astype(jnp.bfloat16)
        dround = dstate.astype(jnp.bfloat16).astype(jnp.float32)
        sround = state.astype(jnp.bfloat16).astype(jnp.float32)
        later_rows = (doc_block == dtag)[:, None, None]
        earlier_rows = (doc_block == tag)[:, None, None]
        value_part = jnp.einsum('hts,the->she', weight.astype(jnp.float32), gf) + jnp.where(later_rows, jnp.einsum('shd,hde->she', kf, dround), 0.0)
        key_part = jnp.einsum('hts,thd->shd', grad_weight.astype(jnp.float32), qf) + jnp.where(later_rows, jnp.einsum('she,hde->shd', vf, dround), 0.0)
        query_part = jnp.einsum('hts,shd->thd', grad_weight.astype(jnp.float32), kf) + jnp.where(earlier_rows, jnp.einsum('the,hde->thd', gf, sround), 0.0)
        query_out = (query_part * feature_slope(raw_query.astype(jnp.float32))).astype(jnp.bfloat16)
        key_out = (key_part * feature_slope(raw_key.astype(jnp.float32))).astype(jnp.bfloat16)
        first_doc = doc_block[0]
        chosen = (doc_block == first_doc)[:, None, None]
        summary = jnp.einsum('thd,the->hde', jnp.where(chosen, qf, 0.0), gf)
        return (combine(carry, (summary, first_doc)), (query_out, key_out, value_part.astype(jnp.bfloat16)))
    items = (split(feat_q), split(feat_k), split(values), doc_float, grad_attn, states, tags, split(queries), split(keys))
    _, (query_grad, key_grad, value_grad) = lax.scan(backward_step, start_state, items, reverse=True)
    shape = (TOKENS, HEADS * HEAD_DIM)
    return (query_grad.reshape(shape), key_grad.reshape(shape), value_grad.reshape(shape), out_proj_grad)
```

```python
import functools
import math

import jax
import jax.numpy as jnp
from jax import lax
from jax.experimental import pallas as pl
from jax.experimental.pallas import tpu as pltpu
from jax.sharding import PartitionSpec as P

HEAD = 128
EPS = 1e-06
PAD = 16
HC = 2
BODY = HC * HEAD
BF = jnp.bfloat16
F32 = jnp.float32
MESH = pl.DeviceIdType.MESH


def feature(x):
    return jnp.where(x > 0, x + 1.0, jnp.exp(jnp.minimum(x, 0.0)))


def slope(x):
    return jnp.where(x > 0, 1.0, jnp.exp(jnp.minimum(x, 0.0)))


def dot(a, b, ca, cb):
    return lax.dot_general(a, b, (((ca,), (cb,)), ((), ())), preferred_element_type=F32)


def layer_kernel(
    dims, q_ref, k_ref, v_ref, go_hbm, w_hbm, gain_ref, doc_ref,
    oq_ref, ok_ref, ov_ref, ow_ref,
    whole, theirs, turned, w_ref, attn_ref, fq_ref, fk_ref, weight_ref, mask_ref, col_ref,
    pair, grad_ref, vp_ref, kp_ref, state, own, oth, ein, eout, far, acc, sent, got,
    lsem, gsem, psem, osem, esem, fsem, ssem, rsem,
):
    n, tp, depth, mrows, width, factor = dims
    rows, feats = q_ref.shape
    chunks = feats // BODY
    me = lax.axis_index("seq")
    j = lax.axis_index("tp")
    x = me % 2
    z = me // 2
    last = depth - 1
    mate = {"seq": me + 1 - 2 * x}
    core = {"tp": j + 1 - 2 * (j % 2)}
    side = {"tp": j + 2 - 4 * (j // 2)}
    partner = {"seq": lax.rem(me + n // 2, n)}
    low_half = z < depth // 2
    odd = j % 2
    lead = odd * (1 - z // (depth // 2)) + (1 - odd) * (z // (depth // 2))
    leads = lead == 1
    trails = lead == 0
    end = (z == 0) | (z == last)
    inner = (z > 0) & (z < last)
    mine_at = pl.ds(pl.multiple_of(x * mrows, mrows), mrows)
    mate_at = pl.ds(pl.multiple_of((1 - x) * mrows, mrows), mrows)

    def rc(src, dst, sems, at, dev):
        return pltpu.make_async_remote_copy(
            src_ref=src, dst_ref=dst, send_sem=sems.at[0, at], recv_sem=sems.at[1, at],
            device_id=dev, device_id_type=MESH,
        )

    load_go = pltpu.make_async_copy(go_hbm, whole.at[0], lsem.at[0])
    load_w = pltpu.make_async_copy(w_hbm, w_ref, lsem.at[1])
    load_go.start()
    load_w.start()

    barrier = pltpu.get_barrier_semaphore()
    fixed = [mate, core, side, partner]
    for dev in fixed:
        pl.semaphore_signal(barrier, inc=1, device_id=dev, device_id_type=MESH)

    @pl.when(z > 0)
    def _():
        pl.semaphore_signal(barrier, inc=1, device_id={"seq": me - 2}, device_id_type=MESH)

    @pl.when(z < last)
    def _():
        pl.semaphore_signal(barrier, inc=1, device_id={"seq": me + 2}, device_id_type=MESH)

    row = doc_ref[...].astype(F32)
    first = row[:, 0:1]
    final = row[:, rows - 1 : rows]
    col_ref[...] = jnp.broadcast_to(row, (HEAD, rows)).T
    for i in range(rows // HEAD):
        cut = slice(i * HEAD, (i + 1) * HEAD)
        at = lax.broadcasted_iota(jnp.int32, (rows, HEAD), 0)
        to = lax.broadcasted_iota(jnp.int32, (rows, HEAD), 1) + i * HEAD
        keep = (at >= to) & (col_ref[...] == row[:, cut])
        mask_ref[:, cut] = jnp.where(keep, 1.0, 0.0).astype(BF)

    sides = (z + depth - 1) // depth + (last - z + depth - 1) // depth
    pl.semaphore_wait(barrier, len(fixed) + sides)
    load_go.wait()

    mine_side = rc(whole.at[0, :, mine_at], whole.at[2, :, mine_at], gsem, 0, side)
    rest_side = rc(whole.at[0, :, mate_at], whole.at[2, :, mate_at], gsem, 1, side)
    swap = rc(whole.at[0, :, mate_at], theirs.at[0], gsem, 2, mate)
    theirs_side = rc(theirs.at[0], theirs.at[2], gsem, 3, side)
    whole_core = rc(whole.at[0], whole.at[1], gsem, 4, core)
    mine_core = rc(whole.at[2, :, mine_at], whole.at[3, :, mine_at], gsem, 5, core)
    rest_core = rc(whole.at[2, :, mate_at], whole.at[3, :, mate_at], gsem, 6, core)
    theirs_core = rc(theirs.at[0], theirs.at[1], gsem, 7, core)
    far_core = rc(theirs.at[2], theirs.at[3], gsem, 8, core)

    def swap_copy(w, c):
        return rc(own.at[w, c], oth.at[w, c], osem, w * chunks + c, mate)

    def carry_copy(w, c):
        return rc(eout.at[w, c], ein.at[w, c], esem, w * chunks + c, {"seq": lax.rem(me + 2 - 4 * w + n, n)})

    def far_copy(c):
        return rc(eout.at[0, c], far.at[c], fsem, c, partner)

    def put(w, c, left, right_at, edge):
        for i in range(HC):
            own[w, c, i * HEAD : (i + 1) * HEAD, :] = dot(left[i], right_at[i], 0, 0).astype(BF)
        own[w, c, BODY:, :] = jnp.broadcast_to(edge, (PAD, HEAD)).astype(BF)
        swap_copy(w, c).start()

    def tag(ref, at):
        return ref[at + (slice(BODY, BODY + 1), slice(None))].astype(F32)

    def body(ref, at):
        return ref[at + (slice(0, BODY), slice(None))].astype(F32)

    def joined(w, c):
        ta, tb = tag(own, (w, c)), tag(oth, (w, c))
        front = x == w
        late_tag = jnp.where(front, tb, ta)
        same = jnp.where(ta == tb, 1.0, 0.0)
        keep_a = jnp.where(front, same, 1.0)
        keep_b = jnp.where(front, 1.0, same)
        return body(own, (w, c)) * keep_a + body(oth, (w, c)) * keep_b, late_tag

    def chunk_at(c):
        return pl.ds(pl.multiple_of(c * BODY, BODY), BODY)

    def near_part(w, c, edge):
        near = jnp.where(x == w, 0.0, jnp.where(tag(oth, (w, c)) == edge, 1.0, 0.0))
        return body(oth, (w, c)) * near

    @pl.when(z == 0)
    def _():
        ein[0] = jnp.zeros(ein.shape[1:], BF)

    @pl.when(z == last)
    def _():
        ein[1] = jnp.zeros(ein.shape[1:], BF)

    @pl.when(low_half)
    def _():
        far[...] = jnp.zeros(far.shape, BF)

    def spread(c):
        swap_copy(0, c).wait_recv()

        @pl.when(z < last)
        def _():
            total, late_tag = joined(0, c)
            eout[0, c, :BODY, :] = total.astype(BF)
            eout[0, c, BODY:, :] = jnp.broadcast_to(late_tag, (PAD, HEAD)).astype(BF)
            carry_copy(0, c).start()

            @pl.when(low_half)
            def _():
                far_copy(c).start()

    def collect(c):
        @pl.when(z > 0)
        def _():
            carry_copy(0, c).wait_recv()

        @pl.when(jnp.logical_not(low_half))
        def _():
            far_copy(c).wait_recv()

        got_one = jnp.where(tag(ein, (0, c)) == first, 1.0, 0.0)
        got_two = jnp.where(tag(far, (c,)) == first, 1.0, 0.0)
        total = near_part(0, c, first) + body(ein, (0, c)) * got_one + body(far, (c,)) * got_two
        state[0, chunk_at(c), :] = total.astype(BF)

    def back(at_z):
        @pl.when(z == at_z)
        def _():
            @pl.loop(0, chunks)
            def _(c):
                swap_copy(1, c).wait_recv()
                if at_z < last:
                    carry_copy(1, c).wait_recv()
                if at_z > 0:
                    total, late_tag = joined(1, c)
                    keep = jnp.where(tag(ein, (1, c)) == late_tag, 1.0, 0.0)
                    eout[1, c, :BODY, :] = (total + body(ein, (1, c)) * keep).astype(BF)
                    eout[1, c, BODY:, :] = jnp.broadcast_to(late_tag, (PAD, HEAD)).astype(BF)
                    carry_copy(1, c).start()
                got_one = jnp.where(tag(ein, (1, c)) == final, 1.0, 0.0)
                total = near_part(1, c, final) + body(ein, (1, c)) * got_one
                state[1, chunk_at(c), :] = total.astype(BF)

    def pair_copy(c):
        return rc(pair.at[c, 0], pair.at[c, 1], psem, c, mate)

    def heads_loop(begin, stop, step):
        @pl.loop(begin, stop)
        def _(h):
            step(h, pl.ds(pl.multiple_of(h * HEAD, HEAD), HEAD))

    def inside(h, at):
        fq = feature(q_ref[:, at].astype(F32)).astype(BF)
        fq_ref[:, at] = fq
        weight = dot(fq, fk_ref[:, at], 1, 1).astype(BF) * mask_ref[...]
        weight_ref[h] = weight
        attn_ref[:, at] = dot(weight, v_ref[:, at], 1, 0)

    def local(c):
        heads_loop(c * HC, (c + 1) * HC, inside)

    def finish(c):
        collect(c)
        for i in range(HC):
            at = slice((c * HC + i) * HEAD, (c * HC + i + 1) * HEAD)
            outer = dot(fq_ref[:, at], state[0, at, :], 1, 0)
            attn = attn_ref[:, at] + jnp.where(col_ref[...] == first, outer, 0.0)
            inv = lax.rsqrt(jnp.mean(attn * attn, axis=-1, keepdims=True) + EPS)
            attn_ref[:, at] = attn
            pair[c, 0, :, i * HEAD : (i + 1) * HEAD] = (attn * inv * gain_ref[:, at]).astype(BF)
        pair_copy(c).start()

    def turn(begin):
        @pl.loop(0, 2)
        def _(i):
            k = begin + 2 * i
            turned[k, 0] = whole[k, :, mine_at].T
            turned[k, 1] = theirs[k].T

    def swapped(cond):
        @pl.when(cond)
        def _():
            swap.wait_recv()
            theirs_side.start()
            theirs_core.start()

    def spread_far(cond):
        @pl.when(cond)
        def _():
            theirs_side.wait_recv()
            far_core.start()

    def from_core(cond):
        @pl.when(cond)
        def _():
            whole_core.wait_recv()
            theirs_core.wait_recv()
            mine_core.wait_recv()
            far_core.wait_recv()

    def partial(c, dest):
        k = jnp.int32(0)
        for b in range(2):
            k = k + (1 << b) * ((dest // (1 << b) + j // (1 << b)) % 2)
        value = dot(turned[k, 0], pair[c, 0], 1, 0) + dot(turned[k, 1], pair[c, 1], 1, 0)
        return value * factor

    def going(w, t):
        return last - t + z if w == 0 else z - last + t

    def chain(w, c, dest, slot):
        return pltpu.make_async_remote_copy(
            src_ref=sent.at[c, dest], dst_ref=got.at[c, slot],
            send_sem=ssem.at[c * depth + dest], recv_sem=rsem.at[c * (depth + 1) + slot],
            device_id={"seq": lax.rem(me + 2 - 4 * w + n, n)}, device_id_type=MESH,
        )

    def slot_of(w, t):
        return depth if (w == 1 and t == last - 1) else going(w, t)

    def on_way(w, t):
        return (z <= t) if w == 0 else (z >= last - t)

    def send_end(c, t):
        for w in range(2):

            @pl.when(z == (0 if w == 0 else last))
            def _():
                dest = going(w, t)
                sent[c, dest] = partial(c, dest).astype(BF)
                chain(w, c, dest, slot_of(w, t)).start()

    def send_inner(c, t):
        for w in range(2):

            @pl.when(on_way(w, t) & inner)
            def _():
                dest = going(w, t)
                acc[...] = partial(c, dest)
                chain(w, c, dest, dest).wait_recv()
                sent[c, dest] = (acc[...] + got[c, dest].astype(F32)).astype(BF)
                chain(w, c, dest, slot_of(w, t)).start()

    def paired(c, cond):
        @pl.when(cond)
        def _():
            pair_copy(c).wait_recv()

    def upstream(c):
        at = slice(c * BODY, (c + 1) * BODY)
        total = None
        for k in range(tp):
            owner = jnp.int32(0)
            for b in range(2):
                owner = owner + (1 << b) * (((k >> b) + j // (1 << b)) % 2)
            start = pl.multiple_of(owner * width, width)
            term = dot(whole[k], w_ref[at, pl.ds(start, width)], 1, 1)
            total = term if total is None else total + term
        left, right = [], []
        for i in range(HC):
            cut = slice(c * BODY + i * HEAD, c * BODY + (i + 1) * HEAD)
            attn = attn_ref[:, cut]
            inv = lax.rsqrt(jnp.mean(attn * attn, axis=-1, keepdims=True) + EPS)
            scaled = total[:, i * HEAD : (i + 1) * HEAD] * gain_ref[:, cut]
            mean = jnp.mean(attn * scaled, axis=-1, keepdims=True)
            grad = (scaled * inv - attn * (inv * inv * inv) * mean).astype(BF)
            grad_ref[:, cut] = grad
            left.append(jnp.where(col_ref[...] == first, fq_ref[:, cut].astype(F32), 0.0).astype(BF))
            right.append(grad)
        put(1, c, left, right, first)

    def inside_back(h, at):
        g = grad_ref[:, at]
        gw = dot(g, v_ref[:, at], 1, 1).astype(BF) * mask_ref[...]
        vp_ref[:, at] = dot(weight_ref[h], g, 0, 0)
        kp_ref[:, at] = dot(gw, fq_ref[:, at], 0, 0)
        outer = dot(g, state[0, at, :], 1, 1)
        qp = dot(gw, fk_ref[:, at], 1, 0) + jnp.where(col_ref[...] == first, outer, 0.0)
        oq_ref[:, at] = (qp * slope(q_ref[:, at].astype(F32))).astype(BF)

    def outside_back(h, at):
        late = col_ref[...] == final
        d = state[1, at, :]
        vp = vp_ref[:, at] + jnp.where(late, dot(fk_ref[:, at], d, 1, 0), 0.0)
        ov_ref[:, at] = vp.astype(BF)
        kp = kp_ref[:, at] + jnp.where(late, dot(v_ref[:, at], d, 1, 1), 0.0)
        ok_ref[:, at] = (kp * slope(k_ref[:, at].astype(F32))).astype(BF)

    whole_core.start()
    mine_side.start()
    for c in range(chunks):
        ats = [slice((c * HC + i) * HEAD, (c * HC + i + 1) * HEAD) for i in range(HC)]
        picked = []
        for at in ats:
            fk = feature(k_ref[:, at].astype(F32))
            fk_ref[:, at] = fk.astype(BF)
            picked.append(jnp.where(col_ref[...] == final, fk, 0.0).astype(BF))
        put(0, c, picked, [v_ref[:, at] for at in ats], final)

    @pl.when(leads)
    def _():
        swap.start()

    local(0)
    pl.loop(0, chunks)(spread)
    local(1)
    finish(0)
    swapped(leads)
    mine_side.wait_recv()
    mine_core.start()
    rest_side.start()
    local(2)
    finish(1)

    @pl.when(trails)
    def _():
        swap.start()

    local(3)
    finish(2)
    finish(3)
    spread_far(leads)
    from_core(trails)
    turn(1 - lead)
    for c in range(2):
        paired(c, end)
        send_end(c, 0)
    rest_side.wait_recv()
    rest_core.start()
    swapped(trails)
    paired(2, end)
    send_end(2, 0)
    paired(0, inner)
    send_inner(0, 1)
    spread_far(trails)
    from_core(leads)
    turn(lead)
    rest_core.wait_recv()
    load_w.wait()
    upstream(0)
    upstream(1)
    paired(3, end)
    send_end(3, 0)
    paired(1, inner)
    send_inner(1, 1)
    upstream(2)
    upstream(3)
    back(last)
    send_end(0, 1)
    send_end(1, 1)
    for c in (2, 3):
        paired(c, inner)
        send_inner(c, 1)
    back(last - 1)
    send_end(2, 1)
    send_end(3, 1)
    heads_loop(0, HC, inside_back)
    for c in range(chunks):
        send_end(c, 2)
    send_inner(0, 2)
    back(last - 2)
    heads_loop(HC, 2 * HC, inside_back)
    send_inner(1, 2)
    heads_loop(2 * HC, 3 * HC, inside_back)
    send_inner(2, 2)
    back(0)
    heads_loop(3 * HC, 4 * HC, inside_back)
    send_inner(3, 2)
    for c in range(chunks):
        ow_ref[:, c * BODY : (c + 1) * BODY] = partial(c, z)
    heads_loop(0, chunks * HC, outside_back)
    for c in range(chunks):
        for w in range(2):

            @pl.when((z > 0) if w == 0 else (z < last))
            def _():
                slot = z if w == 0 else depth
                chain(w, c, z, slot).wait_recv()
                ow_ref[:, c * BODY : (c + 1) * BODY] += got[c, slot].astype(F32)

    for copy in (
        mine_side, rest_side, swap, theirs_side, whole_core, mine_core, rest_core, theirs_core, far_core,
    ):
        copy.wait_send()
    for c in range(chunks):
        pair_copy(c).wait_send()
        for w in range(2):
            swap_copy(w, c).wait_send()

            @pl.when((z < last) if w == 0 else (z > 0))
            def _():
                carry_copy(w, c).wait_send()

            for t in range(last):

                @pl.when(on_way(w, t))
                def _():
                    chain(w, c, going(w, t), slot_of(w, t)).wait_send()

        @pl.when(low_half)
        def _():
            far_copy(c).wait_send()


def local_kernel(queries, keys, values, grad_out, out_weight, norm_gain, doc_ids):
    rows, feats = queries.shape
    n = lax.axis_size("seq")
    tp = lax.axis_size("tp")
    depth = n // 2
    model = out_weight.shape[1]
    width = model // tp
    mrows = model // n
    chunks = feats // BODY
    heads = feats // HEAD
    dims = (n, tp, depth, mrows, width, 1.0 / math.sqrt(rows * n))
    vmem = pl.BlockSpec(memory_space=pltpu.VMEM)
    anyspace = pl.BlockSpec(memory_space=pl.ANY)
    wide = jax.ShapeDtypeStruct((rows, feats), BF)
    summed = pltpu.VMEM((2, chunks, BODY + PAD, HEAD), BF)
    sem = pltpu.SemaphoreType.DMA
    flops = 2 * rows * model * feats * 3
    return pl.pallas_call(
        functools.partial(layer_kernel, dims),
        in_specs=[vmem] * 3 + [anyspace] * 2 + [vmem] * 2,
        out_specs=[vmem] * 4,
        out_shape=[wide] * 3 + [jax.ShapeDtypeStruct((mrows, feats), F32)],
        scratch_shapes=[
            pltpu.VMEM((tp, rows, width), BF),
            pltpu.VMEM((tp, rows, mrows), BF),
            pltpu.VMEM((tp, 2, mrows, rows), BF),
            pltpu.VMEM((feats, model), BF),
            pltpu.VMEM((rows, feats), F32),
            pltpu.VMEM((rows, feats), BF),
            pltpu.VMEM((rows, feats), BF),
            pltpu.VMEM((heads, rows, rows), BF),
            pltpu.VMEM((rows, rows), BF),
            pltpu.VMEM((rows, HEAD), F32),
            pltpu.VMEM((chunks, 2, rows, BODY), BF),
            pltpu.VMEM((rows, feats), BF),
            pltpu.VMEM((rows, feats), F32),
            pltpu.VMEM((rows, feats), F32),
            pltpu.VMEM((2, feats, HEAD), BF),
            summed, summed, summed, summed,
            pltpu.VMEM((chunks, BODY + PAD, HEAD), BF),
            pltpu.VMEM((mrows, BODY), F32),
            pltpu.VMEM((chunks, depth, mrows, BODY), BF),
            pltpu.VMEM((chunks, depth + 1, mrows, BODY), BF),
            sem((2,)),
            sem((2, 9)),
            sem((2, chunks)),
            sem((2, 2 * chunks)),
            sem((2, 2 * chunks)),
            sem((2, chunks)),
            sem((chunks * depth,)),
            sem((chunks * (depth + 1),)),
        ],
        compiler_params=pltpu.CompilerParams(
            collective_id=0, has_side_effects=True, vmem_limit_bytes=60 * 1024 * 1024
        ),
        cost_estimate=pl.CostEstimate(flops=flops, bytes_accessed=flops // 512, transcendentals=0),
        name="layer",
    )(queries, keys, values, grad_out, out_weight, norm_gain[None, :], doc_ids[None, :])


def local_general(queries, keys, values, grad_out, out_weight, norm_gain, doc_ids):
    rows, feats = queries.shape
    n = lax.axis_size("seq")
    me = lax.axis_index("seq")
    heads = feats // HEAD

    def split(array):
        return array.reshape(rows, heads, HEAD)

    def mul(spec, a, b):
        return jnp.einsum(spec, a, b, preferred_element_type=F32)

    q, k = split(queries.astype(F32)), split(keys.astype(F32))
    v, gain = split(values), norm_gain.reshape(heads, HEAD)
    fq, fk = feature(q).astype(BF), feature(k).astype(BF)
    first, final = doc_ids[0], doc_ids[-1]
    early, late = (doc_ids == first)[:, None, None], (doc_ids == final)[:, None, None]
    firsts, finals = lax.all_gather(first, "seq"), lax.all_gather(final, "seq")
    before = (jnp.arange(n) < me) & (finals == first)
    after = (jnp.arange(n) > me) & (firsts == final)

    def over(summary, chosen):
        whole = lax.all_gather(summary, "seq")
        return jnp.sum(jnp.where(chosen[:, None, None, None], whole, 0.0), axis=0).astype(BF)

    at = jnp.arange(rows)
    mask = (at[:, None] >= at[None, :]) & (doc_ids[:, None] == doc_ids[None, :])
    weight = jnp.where(mask, mul("thd,shd->hts", fq, fk), 0.0).astype(BF)
    state = over(mul("shd,she->hde", jnp.where(late, fk, 0), v), before)
    attn = mul("hts,she->the", weight, v)
    attn = attn + jnp.where(early, mul("thd,hde->the", fq, state), 0.0)
    inv = lax.rsqrt(jnp.mean(attn * attn, axis=-1, keepdims=True) + EPS)
    normed = (attn * inv * gain).astype(BF).reshape(rows, feats)
    go = lax.all_gather(grad_out, "tp", axis=1, tiled=True)
    share = mul("tm,tf->mf", go, normed) * (1.0 / math.sqrt(rows * n))
    proj = lax.psum_scatter(share, "seq", scatter_dimension=0, tiled=True)
    scaled = split(mul("tm,fm->tf", go, out_weight)) * gain
    mean = jnp.mean(attn * scaled, axis=-1, keepdims=True)
    grad = (scaled * inv - attn * inv**3 * mean).astype(BF)
    dstate = over(mul("thd,the->hde", jnp.where(early, fq, 0), grad), after)
    gw = jnp.where(mask, mul("the,she->hts", grad, v), 0.0).astype(BF)
    vp = mul("hts,the->she", weight, grad) + jnp.where(late, mul("shd,hde->she", fk, dstate), 0.0)
    kp = mul("hts,thd->shd", gw, fq) + jnp.where(late, mul("she,hde->shd", v, dstate), 0.0)
    qp = mul("hts,shd->thd", gw, fk) + jnp.where(early, mul("the,hde->thd", grad, state), 0.0)
    outs = [qp * slope(q), kp * slope(k), vp]
    return tuple(o.astype(BF).reshape(rows, feats) for o in outs) + (proj,)


def solution(mesh):
    wide = P("seq", "tp")
    in_specs = (wide, wide, wide, wide, P("tp", None), P("tp"), P("seq"))
    local = local_kernel if mesh.shape["seq"] == 8 and mesh.shape["tp"] == 4 else local_general
    return jax.shard_map(
        local, mesh=mesh, in_specs=in_specs, out_specs=(wide,) * 4, check_vma=False
    )
```

```python
import functools
import math

import jax
import jax.numpy as jnp
from jax import lax
from jax.experimental import pallas as pl
from jax.experimental.pallas import tpu as pltpu
from jax.sharding import PartitionSpec as P

HEAD = 128
EPS = 1e-06
PAD = 16
HC = 2
BODY = HC * HEAD
BF = jnp.bfloat16
F32 = jnp.float32
MESH = pl.DeviceIdType.MESH


def feature(x):
    return jnp.where(x > 0, x + 1.0, jnp.exp(jnp.minimum(x, 0.0)))


def slope(x):
    return jnp.where(x > 0, 1.0, jnp.exp(jnp.minimum(x, 0.0)))


def dot(a, b, ca, cb):
    return lax.dot_general(a, b, (((ca,), (cb,)), ((), ())), preferred_element_type=F32)


def layer_kernel(
    dims, q_ref, k_ref, v_ref, go_hbm, w_hbm, gain_ref, doc_ref,
    oq_ref, ok_ref, ov_ref, ow_ref,
    whole, theirs, turned, w_ref, attn_ref, fq_ref, fk_ref, weight_ref, mask_ref, col_ref,
    pair, grad_ref, vp_ref, kp_ref, state, own, oth, ein, eout, acc, sent, got,
    lsem, gsem, psem, osem, esem, hsem, ssem, rsem,
):
    n, tp, depth, mrows, width, factor = dims
    rows, feats = q_ref.shape
    chunks = feats // BODY
    spans = [slice(0, HEAD), slice(HEAD, BODY)] + [slice(c * BODY, (c + 1) * BODY) for c in range(1, chunks)]
    pieces = len(spans)
    me = lax.axis_index("seq")
    j = lax.axis_index("tp")
    x = me % 2
    z = me // 2
    last = depth - 1
    mate = {"seq": me + 1 - 2 * x}
    core = {"tp": j + 1 - 2 * (j % 2)}
    side = {"tp": j + 2 - 4 * (j // 2)}
    odd = j % 2
    lead = odd * (1 - z // (depth // 2)) + (1 - odd) * (z // (depth // 2))
    end = (z == 0) | (z == last)
    inner = (z > 0) & (z < last)
    mine_at = pl.ds(pl.multiple_of(x * mrows, mrows), mrows)
    mate_at = pl.ds(pl.multiple_of((1 - x) * mrows, mrows), mrows)

    def rc(src, dst, sems, at, dev):
        return pltpu.make_async_remote_copy(
            src_ref=src, dst_ref=dst, send_sem=sems.at[0, at], recv_sem=sems.at[1, at],
            device_id=dev, device_id_type=MESH,
        )

    load_go = pltpu.make_async_copy(go_hbm, whole.at[0], lsem.at[0])
    load_w = pltpu.make_async_copy(w_hbm, w_ref, lsem.at[1])
    load_go.start()
    load_w.start()

    barrier = pltpu.get_barrier_semaphore()
    fixed = [mate, core, side]
    for dev in fixed:
        pl.semaphore_signal(barrier, inc=1, device_id=dev, device_id_type=MESH)

    @pl.when(z > 0)
    def _():
        pl.semaphore_signal(barrier, inc=1, device_id={"seq": me - 2}, device_id_type=MESH)

    @pl.when(z < last)
    def _():
        pl.semaphore_signal(barrier, inc=1, device_id={"seq": me + 2}, device_id_type=MESH)

    row = doc_ref[...].astype(F32)
    first = row[:, 0:1]
    final = row[:, rows - 1 : rows]
    col_ref[...] = jnp.broadcast_to(row, (HEAD, rows)).T
    for i in range(rows // HEAD):
        cut = slice(i * HEAD, (i + 1) * HEAD)
        at = lax.broadcasted_iota(jnp.int32, (rows, HEAD), 0)
        to = lax.broadcasted_iota(jnp.int32, (rows, HEAD), 1) + i * HEAD
        keep = (at >= to) & (col_ref[...] == row[:, cut])
        mask_ref[:, cut] = jnp.where(keep, 1.0, 0.0).astype(BF)

    sides = (z + depth - 1) // depth + (last - z + depth - 1) // depth
    pl.semaphore_wait(barrier, len(fixed) + sides)
    load_go.wait()

    half = rows // 2
    theirs_first = pl.ds(pl.multiple_of(lead * half, half), half)
    mine_first = pl.ds(pl.multiple_of((1 - lead) * half, half), half)
    core_one = rc(whole.at[0, theirs_first], whole.at[1, theirs_first], gsem, 24, core)
    core_two = rc(whole.at[0, mine_first], whole.at[1, mine_first], gsem, 25, core)

    class Block:
        def __init__(self, p, offset, size, slot):
            k = 1 - lead if p == 0 else lead
            part = pl.ds(pl.multiple_of((1 - lead) * half + offset, size), size)
            flip = 1 - k
            self.k = k
            names = ("swap", "mine_side", "rest_side", "theirs_side", "mine_core", "rest_core", "theirs_core", "far_core")
            ends = (
                (whole.at[k, part, mate_at], theirs.at[k, part], mate),
                (whole.at[k, part, mine_at], whole.at[k + 2, part, mine_at], side),
                (whole.at[k, part, mate_at], whole.at[k + 2, part, mate_at], side),
                (theirs.at[k, part], theirs.at[k + 2, part], side),
                (whole.at[k + 2, part, mine_at], whole.at[flip + 2, part, mine_at], core),
                (whole.at[k + 2, part, mate_at], whole.at[flip + 2, part, mate_at], core),
                (theirs.at[k, part], theirs.at[flip, part], core),
                (theirs.at[k + 2, part], theirs.at[flip + 2, part], core),
            )
            self.all = []
            for i, (name, (src, dst, dev)) in enumerate(zip(names, ends)):
                copy = rc(src, dst, gsem, slot * 8 + i, dev)
                setattr(self, name, copy)
                self.all.append(copy)

    early, more, later = Block(0, 0, half // 2, 0), Block(0, half // 2, half // 2, 1), Block(1, 0, half, 2)

    def swap_copy(w, c):
        return rc(own.at[w, c], oth.at[w, c], osem, w * chunks + c, mate)

    def carry_copy(w, c):
        return rc(eout.at[w, c], ein.at[w, c], esem, w * chunks + c, {"seq": lax.rem(me + 2 - 4 * w + n, n)})

    def put(w, c, left, right_at, edge):
        for i in range(HC):
            own[w, c, i * HEAD : (i + 1) * HEAD, :] = dot(left[i], right_at[i], 0, 0).astype(BF)
        own[w, c, BODY:, :] = jnp.broadcast_to(edge, (PAD, HEAD)).astype(BF)
        swap_copy(w, c).start()

    def share_copy(c):
        return rc(ein.at[1, c], ein.at[1, c], hsem, c, mate)

    def tag(ref, at):
        return ref[at + (slice(BODY, BODY + 1), slice(None))].astype(F32)

    def body(ref, at):
        return ref[at + (slice(0, BODY), slice(None))].astype(F32)

    def joined(w, c):
        ta, tb = tag(own, (w, c)), tag(oth, (w, c))
        front = x == w
        late_tag = jnp.where(front, tb, ta)
        same = jnp.where(ta == tb, 1.0, 0.0)
        keep_a = jnp.where(front, same, 1.0)
        keep_b = jnp.where(front, 1.0, same)
        return body(own, (w, c)) * keep_a + body(oth, (w, c)) * keep_b, late_tag

    def chunk_at(c):
        return pl.ds(pl.multiple_of(c * BODY, BODY), BODY)

    def near_part(w, c, edge):
        near = jnp.where(x == w, 0.0, jnp.where(tag(oth, (w, c)) == edge, 1.0, 0.0))
        return body(oth, (w, c)) * near

    @pl.when(z == 0)
    def _():
        ein[0] = jnp.zeros(ein.shape[1:], BF)

    @pl.when(z == last)
    def _():
        ein[1] = jnp.zeros(ein.shape[1:], BF)

    def carry(c):
        swap_copy(0, c).wait_recv()

        @pl.when(z > 0)
        def _():
            carry_copy(0, c).wait_recv()

        @pl.when(z < last)
        def _():
            total, late_tag = joined(0, c)
            keep = jnp.where(tag(ein, (0, c)) == late_tag, 1.0, 0.0)
            eout[0, c, :BODY, :] = (total + body(ein, (0, c)) * keep).astype(BF)
            eout[0, c, BODY:, :] = jnp.broadcast_to(late_tag, (PAD, HEAD)).astype(BF)
            carry_copy(0, c).start()

        got_one = jnp.where(tag(ein, (0, c)) == first, 1.0, 0.0)
        total = near_part(0, c, first) + body(ein, (0, c)) * got_one
        state[0, chunk_at(c), :] = total.astype(BF)

    def carry_at(at_z, c):
        @pl.when(z == at_z)
        def _():
            carry(c)

    def back(at_z):
        @pl.when(z == at_z)
        def _():
            if at_z < last:

                @pl.loop(0, chunks // 2)
                def _(i):
                    carry_copy(1, 2 * i + x).wait_recv()
                    share_copy(2 * i + x).start()

            @pl.loop(0, chunks)
            def _(c):
                swap_copy(1, c).wait_recv()
                if at_z < last:

                    @pl.when(c % 2 != x)
                    def _():
                        share_copy(c).wait_recv()

                if at_z > 0:

                    @pl.when(c % 2 == x)
                    def _():
                        total, late_tag = joined(1, c)
                        keep = jnp.where(tag(ein, (1, c)) == late_tag, 1.0, 0.0)
                        eout[1, c, :BODY, :] = (total + body(ein, (1, c)) * keep).astype(BF)
                        eout[1, c, BODY:, :] = jnp.broadcast_to(late_tag, (PAD, HEAD)).astype(BF)
                        carry_copy(1, c).start()

                got_one = jnp.where(tag(ein, (1, c)) == final, 1.0, 0.0)
                total = near_part(1, c, final) + body(ein, (1, c)) * got_one
                state[1, chunk_at(c), :] = total.astype(BF)

    def pair_copy(p):
        return rc(pair.at[0, :, spans[p]], pair.at[1, :, spans[p]], psem, p, mate)

    def heads_loop(begin, stop, step):
        @pl.loop(begin, stop)
        def _(h):
            step(h, pl.ds(pl.multiple_of(h * HEAD, HEAD), HEAD))

    def inside(h, at):
        fq = feature(q_ref[:, at].astype(F32)).astype(BF)
        fq_ref[:, at] = fq
        weight = dot(fq, fk_ref[:, at], 1, 1).astype(BF) * mask_ref[...]
        weight_ref[h] = weight
        attn_ref[:, at] = dot(weight, v_ref[:, at], 1, 0)

    def local(c):
        heads_loop(c * HC, (c + 1) * HC, inside)

    def finish(c):
        for i in range(HC):
            at = slice((c * HC + i) * HEAD, (c * HC + i + 1) * HEAD)
            outer = dot(fq_ref[:, at], state[0, at, :], 1, 0)
            attn = attn_ref[:, at] + jnp.where(col_ref[...] == first, outer, 0.0)
            inv = lax.rsqrt(jnp.mean(attn * attn, axis=-1, keepdims=True) + EPS)
            attn_ref[:, at] = attn
            pair[0, :, at] = (attn * inv * gain_ref[:, at]).astype(BF)
            if c == 0:
                pair_copy(i).start()
        if c > 0:
            pair_copy(c + 1).start()

    def turn(block):
        @pl.loop(0, 2)
        def _(i):
            k = block.k + 2 * i
            turned[k, 0] = whole[k, :, mine_at].T
            turned[k, 1] = theirs[k].T

    def swapped(block):
        block.swap.wait_recv()
        block.theirs_side.start()
        block.theirs_core.start()

    def mine_here(block):
        block.mine_side.wait_recv()
        block.mine_core.start()

    def rest_here(block):
        block.rest_side.wait_recv()
        block.rest_core.start()

    def theirs_here(block):
        block.theirs_side.wait_recv()
        block.far_core.start()

    def lead_ready():
        for block in (early, more):
            theirs_here(block)
        for block in (early, more):
            block.theirs_core.wait_recv()
            block.mine_core.wait_recv()
            block.far_core.wait_recv()
        core_two.wait_recv()
        turn(early)

    def partial(p, dest):
        k = jnp.int32(0)
        for b in range(2):
            k = k + (1 << b) * ((dest // (1 << b) + j // (1 << b)) % 2)
        value = dot(turned[k, 0], pair[0, :, spans[p]], 1, 0) + dot(turned[k, 1], pair[1, :, spans[p]], 1, 0)
        return value * factor

    def going(w, t):
        return last - t + z if w == 0 else z - last + t

    def chain(w, p, dest, slot):
        return pltpu.make_async_remote_copy(
            src_ref=sent.at[dest, :, spans[p]], dst_ref=got.at[slot, :, spans[p]],
            send_sem=ssem.at[p * depth + dest], recv_sem=rsem.at[p * (depth + 1) + slot],
            device_id={"seq": lax.rem(me + 2 - 4 * w + n, n)}, device_id_type=MESH,
        )

    def slot_of(w, t):
        return depth if (w == 1 and t == last - 1) else going(w, t)

    def on_way(w, t):
        return (z <= t) if w == 0 else (z >= last - t)

    def send_end(p, t):
        for w in range(2):

            @pl.when(z == (0 if w == 0 else last))
            def _():
                dest = going(w, t)
                sent[dest, :, spans[p]] = partial(p, dest).astype(BF)
                chain(w, p, dest, slot_of(w, t)).start()

    def relay(p, w, t, when):
        @pl.when(when)
        def _():
            dest = going(w, t)
            size = spans[p].stop - spans[p].start
            acc[:, :size] = partial(p, dest)
            chain(w, p, dest, dest).wait_recv()
            sent[dest, :, spans[p]] = (acc[:, :size] + got[dest, :, spans[p]].astype(F32)).astype(BF)
            chain(w, p, dest, slot_of(w, t)).start()

    def onward(p, t):
        relay(p, 0, t, z == 1)
        relay(p, 1, t, z == last - 1)

    def returning(p):
        relay(p, 1, last - 1, z == 1)
        relay(p, 0, last - 1, z == last - 1)

    def paired(p, cond):
        @pl.when(cond)
        def _():
            pair_copy(p).wait_recv()

    def upstream(c):
        at = slice(c * BODY, (c + 1) * BODY)
        total = None
        for k in range(tp):
            owner = jnp.int32(0)
            for b in range(2):
                owner = owner + (1 << b) * (((k >> b) + j // (1 << b)) % 2)
            start = pl.multiple_of(owner * width, width)
            term = dot(whole[k], w_ref[at, pl.ds(start, width)], 1, 1)
            total = term if total is None else total + term
        left, right = [], []
        for i in range(HC):
            cut = slice(c * BODY + i * HEAD, c * BODY + (i + 1) * HEAD)
            attn = attn_ref[:, cut]
            inv = lax.rsqrt(jnp.mean(attn * attn, axis=-1, keepdims=True) + EPS)
            scaled = total[:, i * HEAD : (i + 1) * HEAD] * gain_ref[:, cut]
            mean = jnp.mean(attn * scaled, axis=-1, keepdims=True)
            grad = (scaled * inv - attn * (inv * inv * inv) * mean).astype(BF)
            grad_ref[:, cut] = grad
            left.append(jnp.where(col_ref[...] == first, fq_ref[:, cut].astype(F32), 0.0).astype(BF))
            right.append(grad)
        put(1, c, left, right, first)

    def inside_back(h, at):
        g = grad_ref[:, at]
        gw = dot(g, v_ref[:, at], 1, 1).astype(BF) * mask_ref[...]
        vp_ref[:, at] = dot(weight_ref[h], g, 0, 0)
        kp_ref[:, at] = dot(gw, fq_ref[:, at], 0, 0)
        outer = dot(g, state[0, at, :], 1, 1)
        qp = dot(gw, fk_ref[:, at], 1, 0) + jnp.where(col_ref[...] == first, outer, 0.0)
        oq_ref[:, at] = (qp * slope(q_ref[:, at].astype(F32))).astype(BF)

    def outside_back(h, at):
        late = col_ref[...] == final
        d = state[1, at, :]
        vp = vp_ref[:, at] + jnp.where(late, dot(fk_ref[:, at], d, 1, 0), 0.0)
        ov_ref[:, at] = vp.astype(BF)
        kp = kp_ref[:, at] + jnp.where(late, dot(v_ref[:, at], d, 1, 1), 0.0)
        ok_ref[:, at] = (kp * slope(k_ref[:, at].astype(F32))).astype(BF)

    def keys_put(c):
        ats = [slice((c * HC + i) * HEAD, (c * HC + i + 1) * HEAD) for i in range(HC)]
        picked = []
        for at in ats:
            fk = feature(k_ref[:, at].astype(F32))
            fk_ref[:, at] = fk.astype(BF)
            picked.append(jnp.where(col_ref[...] == final, fk, 0.0).astype(BF))
        put(0, c, picked, [v_ref[:, at] for at in ats], final)

    core_one.start()
    core_two.start()
    keys_put(0)

    @pl.when(lead == 0)
    def _():
        core_one.wait_recv()

    for block in (early, more):
        block.mine_side.start()
        block.swap.start()
    for c in range(1, chunks):
        keys_put(c)
    local(0)
    carry_at(0, 0)
    local(1)
    carry_at(1, 0)
    local(2)
    swapped(early)
    carry_at(2, 0)
    local(3)
    mine_here(early)
    mine_here(more)
    swapped(more)

    @pl.when(lead == 1)
    def _():
        core_one.wait_recv()

    later.mine_side.start()
    for block in (early, more, later):
        block.rest_side.start()
    carry_at(3, 0)
    finish(0)
    carry(1)
    finish(1)

    @pl.when(z < last)
    def _():
        for c in (2, 3):
            carry(c)
            finish(c)
        later.swap.start()

    lead_ready()
    paired(0, end)
    send_end(0, 0)
    paired(1, end)
    send_end(1, 0)

    @pl.when(z == last)
    def _():
        for c in (2, 3):
            carry(c)
            finish(c)
        later.swap.start()

    send_end(0, 2)
    send_end(1, 2)
    mine_here(later)
    paired(0, inner)
    onward(0, 1)
    paired(1, inner)
    onward(1, 1)
    paired(2, end)
    send_end(2, 0)
    paired(3, end)
    send_end(3, 0)
    load_w.wait()
    for block in (early, more, later):
        rest_here(block)
    for block in (early, more, later):
        block.rest_core.wait_recv()
    later.mine_core.wait_recv()
    upstream(0)
    paired(4, end)
    send_end(4, 0)
    paired(2, inner)
    onward(2, 1)
    upstream(1)
    paired(3, inner)
    onward(3, 1)
    swapped(later)
    send_end(2, 2)
    upstream(2)
    paired(4, inner)
    onward(4, 1)
    theirs_here(later)
    later.theirs_core.wait_recv()
    later.far_core.wait_recv()
    turn(later)
    send_end(0, 1)
    send_end(1, 1)
    upstream(3)
    back(last)
    send_end(2, 1)
    send_end(3, 1)
    send_end(4, 1)
    send_end(3, 2)
    send_end(4, 2)
    for p in range(pieces):
        returning(p)
    heads_loop(0, 2 * HC, inside_back)
    onward(0, 2)
    onward(1, 2)
    back(last - 1)
    heads_loop(2 * HC, 3 * HC, inside_back)
    onward(2, 2)
    heads_loop(3 * HC, 4 * HC, inside_back)
    back(last - 2)
    onward(3, 2)
    for p in range(pieces):
        ow_ref[:, spans[p]] = partial(p, z)
    back(0)
    onward(4, 2)
    heads_loop(0, chunks * HC, outside_back)
    for p in range(pieces):
        for w in range(2):

            @pl.when((z > 0) if w == 0 else (z < last))
            def _():
                slot = z if w == 0 else depth
                chain(w, p, z, slot).wait_recv()
                ow_ref[:, spans[p]] += got[slot, :, spans[p]].astype(F32)

    for copy in [core_one, core_two] + early.all + more.all + later.all:
        copy.wait_send()
    for c in range(chunks):
        swap_copy(0, c).wait_send()
        swap_copy(1, c).wait_send()

        @pl.when(z < last)
        def _():
            carry_copy(0, c).wait_send()

        @pl.when((z > 0) & (x == c % 2))
        def _():
            carry_copy(1, c).wait_send()

        @pl.when((z < last) & (x == c % 2))
        def _():
            share_copy(c).wait_send()

    for p in range(pieces):
        pair_copy(p).wait_send()
        for w in range(2):
            for t in range(last):

                @pl.when(on_way(w, t))
                def _():
                    chain(w, p, going(w, t), slot_of(w, t)).wait_send()


def local_kernel(queries, keys, values, grad_out, out_weight, norm_gain, doc_ids):
    rows, feats = queries.shape
    n = lax.axis_size("seq")
    tp = lax.axis_size("tp")
    depth = n // 2
    model = out_weight.shape[1]
    width = model // tp
    mrows = model // n
    chunks = feats // BODY
    heads = feats // HEAD
    dims = (n, tp, depth, mrows, width, 1.0 / math.sqrt(rows * n))
    vmem = pl.BlockSpec(memory_space=pltpu.VMEM)
    anyspace = pl.BlockSpec(memory_space=pl.ANY)
    wide = jax.ShapeDtypeStruct((rows, feats), BF)
    summed = pltpu.VMEM((2, chunks, BODY + PAD, HEAD), BF)
    sem = pltpu.SemaphoreType.DMA
    flops = 2 * rows * model * feats * 3
    return pl.pallas_call(
        functools.partial(layer_kernel, dims),
        in_specs=[vmem] * 3 + [anyspace] * 2 + [vmem] * 2,
        out_specs=[vmem] * 4,
        out_shape=[wide] * 3 + [jax.ShapeDtypeStruct((mrows, feats), F32)],
        scratch_shapes=[
            pltpu.VMEM((tp, rows, width), BF),
            pltpu.VMEM((tp, rows, mrows), BF),
            pltpu.VMEM((tp, 2, mrows, rows), BF),
            pltpu.VMEM((feats, model), BF),
            pltpu.VMEM((rows, feats), F32),
            pltpu.VMEM((rows, feats), BF),
            pltpu.VMEM((rows, feats), BF),
            pltpu.VMEM((heads, rows, rows), BF),
            pltpu.VMEM((rows, rows), BF),
            pltpu.VMEM((rows, HEAD), F32),
            pltpu.VMEM((2, rows, feats), BF),
            pltpu.VMEM((rows, feats), BF),
            pltpu.VMEM((rows, feats), F32),
            pltpu.VMEM((rows, feats), F32),
            pltpu.VMEM((2, feats, HEAD), BF),
            summed, summed, summed, summed,
            pltpu.VMEM((mrows, BODY), F32),
            pltpu.VMEM((depth, mrows, feats), BF),
            pltpu.VMEM((depth + 1, mrows, feats), BF),
            sem((2,)),
            sem((2, 26)),
            sem((2, chunks + 1)),
            sem((2, 2 * chunks)),
            sem((2, 2 * chunks)),
            sem((2, chunks)),
            sem(((chunks + 1) * depth,)),
            sem(((chunks + 1) * (depth + 1),)),
        ],
        compiler_params=pltpu.CompilerParams(
            collective_id=0, has_side_effects=True, vmem_limit_bytes=60 * 1024 * 1024
        ),
        cost_estimate=pl.CostEstimate(flops=flops, bytes_accessed=flops // 512, transcendentals=0),
        name="layer",
    )(queries, keys, values, grad_out, out_weight, norm_gain[None, :], doc_ids[None, :])


def local_general(queries, keys, values, grad_out, out_weight, norm_gain, doc_ids):
    rows, feats = queries.shape
    n = lax.axis_size("seq")
    me = lax.axis_index("seq")
    heads = feats // HEAD

    def split(array):
        return array.reshape(rows, heads, HEAD)

    def mul(spec, a, b):
        return jnp.einsum(spec, a, b, preferred_element_type=F32)

    q, k = split(queries.astype(F32)), split(keys.astype(F32))
    v, gain = split(values), norm_gain.reshape(heads, HEAD)
    fq, fk = feature(q).astype(BF), feature(k).astype(BF)
    first, final = doc_ids[0], doc_ids[-1]
    early, late = (doc_ids == first)[:, None, None], (doc_ids == final)[:, None, None]
    firsts, finals = lax.all_gather(first, "seq"), lax.all_gather(final, "seq")
    before = (jnp.arange(n) < me) & (finals == first)
    after = (jnp.arange(n) > me) & (firsts == final)

    def over(summary, chosen):
        whole = lax.all_gather(summary, "seq")
        return jnp.sum(jnp.where(chosen[:, None, None, None], whole, 0.0), axis=0).astype(BF)

    at = jnp.arange(rows)
    mask = (at[:, None] >= at[None, :]) & (doc_ids[:, None] == doc_ids[None, :])
    weight = jnp.where(mask, mul("thd,shd->hts", fq, fk), 0.0).astype(BF)
    state = over(mul("shd,she->hde", jnp.where(late, fk, 0), v), before)
    attn = mul("hts,she->the", weight, v)
    attn = attn + jnp.where(early, mul("thd,hde->the", fq, state), 0.0)
    inv = lax.rsqrt(jnp.mean(attn * attn, axis=-1, keepdims=True) + EPS)
    normed = (attn * inv * gain).astype(BF).reshape(rows, feats)
    go = lax.all_gather(grad_out, "tp", axis=1, tiled=True)
    share = mul("tm,tf->mf", go, normed) * (1.0 / math.sqrt(rows * n))
    proj = lax.psum_scatter(share, "seq", scatter_dimension=0, tiled=True)
    scaled = split(mul("tm,fm->tf", go, out_weight)) * gain
    mean = jnp.mean(attn * scaled, axis=-1, keepdims=True)
    grad = (scaled * inv - attn * inv**3 * mean).astype(BF)
    dstate = over(mul("thd,the->hde", jnp.where(early, fq, 0), grad), after)
    gw = jnp.where(mask, mul("the,she->hts", grad, v), 0.0).astype(BF)
    vp = mul("hts,the->she", weight, grad) + jnp.where(late, mul("shd,hde->she", fk, dstate), 0.0)
    kp = mul("hts,thd->shd", gw, fq) + jnp.where(late, mul("she,hde->shd", v, dstate), 0.0)
    qp = mul("hts,shd->thd", gw, fk) + jnp.where(early, mul("the,hde->thd", grad, state), 0.0)
    outs = [qp * slope(q), kp * slope(k), vp]
    return tuple(o.astype(BF).reshape(rows, feats) for o in outs) + (proj,)


def solution(mesh):
    wide = P("seq", "tp")
    in_specs = (wide, wide, wide, wide, P("tp", None), P("tp"), P("seq"))
    local = local_kernel if mesh.shape["seq"] == 8 and mesh.shape["tp"] == 4 else local_general
    return jax.shard_map(
        local, mesh=mesh, in_specs=in_specs, out_specs=(wide,) * 4, check_vma=False
    )
```

```python
import functools
import math

import jax
import jax.numpy as jnp
from jax import lax
from jax.experimental import pallas as pl
from jax.experimental.pallas import tpu as pltpu
from jax.sharding import PartitionSpec as P

HEAD = 128
EPS = 1e-06
PAD = 16
HC = 2
BODY = HC * HEAD
BF = jnp.bfloat16
F32 = jnp.float32
MESH = pl.DeviceIdType.MESH


def feature(x):
    return jnp.where(x > 0, x + 1.0, jnp.exp(jnp.minimum(x, 0.0)))


def slope(x):
    return jnp.where(x > 0, 1.0, jnp.exp(jnp.minimum(x, 0.0)))


def dot(a, b, ca, cb):
    return lax.dot_general(a, b, (((ca,), (cb,)), ((), ())), preferred_element_type=F32)


def layer_kernel(
    dims, q_ref, k_ref, v_ref, go_hbm, w_hbm, gain_ref, doc_ref,
    oq_ref, ok_ref, ov_ref, ow_ref,
    whole, theirs, turned, w_ref, attn_ref, fq_ref, fk_ref, weight_ref, mask_ref, col_ref,
    pair, grad_ref, vp_ref, kp_ref, state, own, oth, ein, eout, acc, sent, got,
    lsem, gsem, psem, osem, esem, hsem, ssem, rsem,
):
    n, tp, depth, mrows, width, factor = dims
    rows, feats = q_ref.shape
    chunks = feats // BODY
    pieces = chunks + 1

    def span(p):
        if isinstance(p, int) and p < 2:
            return pl.ds(p * HEAD, HEAD)
        return pl.ds(pl.multiple_of((p - 1) * BODY, BODY), BODY)

    me = lax.axis_index("seq")
    j = lax.axis_index("tp")
    x = me % 2
    z = me // 2
    last = depth - 1
    mate = {"seq": me + 1 - 2 * x}
    core = {"tp": j + 1 - 2 * (j % 2)}
    side = {"tp": j + 2 - 4 * (j // 2)}
    odd = j % 2
    lead = odd * (1 - z // (depth // 2)) + (1 - odd) * (z // (depth // 2))
    end = (z == 0) | (z == last)
    inner = (z > 0) & (z < last)
    mine_at = pl.ds(pl.multiple_of(x * mrows, mrows), mrows)
    mate_at = pl.ds(pl.multiple_of((1 - x) * mrows, mrows), mrows)

    def rc(src, dst, sems, at, dev):
        return pltpu.make_async_remote_copy(
            src_ref=src, dst_ref=dst, send_sem=sems.at[0, at], recv_sem=sems.at[1, at],
            device_id=dev, device_id_type=MESH,
        )

    load_go = pltpu.make_async_copy(go_hbm, whole.at[0], lsem.at[0])
    load_w = pltpu.make_async_copy(w_hbm, w_ref, lsem.at[1])
    load_go.start()
    load_w.start()

    barrier = pltpu.get_barrier_semaphore()
    fixed = [mate, core, side]
    for dev in fixed:
        pl.semaphore_signal(barrier, inc=1, device_id=dev, device_id_type=MESH)

    @pl.when(z > 0)
    def _():
        pl.semaphore_signal(barrier, inc=1, device_id={"seq": me - 2}, device_id_type=MESH)

    @pl.when(z < last)
    def _():
        pl.semaphore_signal(barrier, inc=1, device_id={"seq": me + 2}, device_id_type=MESH)

    row = doc_ref[...].astype(F32)
    first = row[:, 0:1]
    final = row[:, rows - 1 : rows]
    col_ref[...] = jnp.broadcast_to(row, (HEAD, rows)).T
    for i in range(rows // HEAD):
        cut = slice(i * HEAD, (i + 1) * HEAD)
        at = lax.broadcasted_iota(jnp.int32, (rows, HEAD), 0)
        to = lax.broadcasted_iota(jnp.int32, (rows, HEAD), 1) + i * HEAD
        keep = (at >= to) & (col_ref[...] == row[:, cut])
        mask_ref[:, cut] = jnp.where(keep, 1.0, 0.0).astype(BF)

    sides = (z + depth - 1) // depth + (last - z + depth - 1) // depth
    pl.semaphore_wait(barrier, len(fixed) + sides)
    load_go.wait()

    half = rows // 2
    theirs_first = pl.ds(pl.multiple_of(lead * half, half), half)
    mine_first = pl.ds(pl.multiple_of((1 - lead) * half, half), half)
    core_one = rc(whole.at[0, theirs_first], whole.at[1, theirs_first], gsem, 24, core)
    core_two = rc(whole.at[0, mine_first], whole.at[1, mine_first], gsem, 25, core)

    class Block:
        def __init__(self, p, offset, size, slot):
            k = 1 - lead if p == 0 else lead
            part = pl.ds(pl.multiple_of((1 - lead) * half + offset, size), size)
            flip = 1 - k
            self.k = k
            names = ("swap", "mine_side", "rest_side", "theirs_side", "mine_core", "rest_core", "theirs_core", "far_core")
            ends = (
                (whole.at[k, part, mate_at], theirs.at[k, part], mate),
                (whole.at[k, part, mine_at], whole.at[k + 2, part, mine_at], side),
                (whole.at[k, part, mate_at], whole.at[k + 2, part, mate_at], side),
                (theirs.at[k, part], theirs.at[k + 2, part], side),
                (whole.at[k + 2, part, mine_at], whole.at[flip + 2, part, mine_at], core),
                (whole.at[k + 2, part, mate_at], whole.at[flip + 2, part, mate_at], core),
                (theirs.at[k, part], theirs.at[flip, part], core),
                (theirs.at[k + 2, part], theirs.at[flip + 2, part], core),
            )
            self.all = []
            for i, (name, (src, dst, dev)) in enumerate(zip(names, ends)):
                copy = rc(src, dst, gsem, slot * 8 + i, dev)
                setattr(self, name, copy)
                self.all.append(copy)

    early, more, later = Block(0, 0, half // 2, 0), Block(0, half // 2, half // 2, 1), Block(1, 0, half, 2)

    def swap_copy(w, c):
        return rc(own.at[w, c], oth.at[w, c], osem, w * chunks + c, mate)

    def carry_copy(w, c):
        return rc(eout.at[w, c], ein.at[w, c], esem, w * chunks + c, {"seq": lax.rem(me + 2 - 4 * w + n, n)})

    def put(w, c, left, right_at, edge):
        for i in range(HC):
            own[w, c, i * HEAD : (i + 1) * HEAD, :] = dot(left[i], right_at[i], 0, 0).astype(BF)
        own[w, c, BODY:, :] = jnp.broadcast_to(edge, (PAD, HEAD)).astype(BF)
        swap_copy(w, c).start()

    def share_copy(c):
        return rc(ein.at[1, c], ein.at[1, c], hsem, c, mate)

    def tag(ref, at):
        return ref[at + (slice(BODY, BODY + 1), slice(None))].astype(F32)

    def body(ref, at):
        return ref[at + (slice(0, BODY), slice(None))].astype(F32)

    def joined(w, c):
        ta, tb = tag(own, (w, c)), tag(oth, (w, c))
        front = x == w
        late_tag = jnp.where(front, tb, ta)
        same = jnp.where(ta == tb, 1.0, 0.0)
        keep_a = jnp.where(front, same, 1.0)
        keep_b = jnp.where(front, 1.0, same)
        return body(own, (w, c)) * keep_a + body(oth, (w, c)) * keep_b, late_tag

    def chunk_at(c):
        return pl.ds(pl.multiple_of(c * BODY, BODY), BODY)

    def near_part(w, c, edge):
        near = jnp.where(x == w, 0.0, jnp.where(tag(oth, (w, c)) == edge, 1.0, 0.0))
        return body(oth, (w, c)) * near

    @pl.when(z == 0)
    def _():
        ein[0] = jnp.zeros(ein.shape[1:], BF)

    @pl.when(z == last)
    def _():
        ein[1] = jnp.zeros(ein.shape[1:], BF)

    def carry(c):
        swap_copy(0, c).wait_recv()

        @pl.when(z > 0)
        def _():
            carry_copy(0, c).wait_recv()

        @pl.when(z < last)
        def _():
            total, late_tag = joined(0, c)
            keep = jnp.where(tag(ein, (0, c)) == late_tag, 1.0, 0.0)
            eout[0, c, :BODY, :] = (total + body(ein, (0, c)) * keep).astype(BF)
            eout[0, c, BODY:, :] = jnp.broadcast_to(late_tag, (PAD, HEAD)).astype(BF)
            carry_copy(0, c).start()

        got_one = jnp.where(tag(ein, (0, c)) == first, 1.0, 0.0)
        total = near_part(0, c, first) + body(ein, (0, c)) * got_one
        state[0, chunk_at(c), :] = total.astype(BF)

    def carry_at(at_z, c):
        @pl.when(z == at_z)
        def _():
            carry(c)

    def back(at_z):
        @pl.when(z == at_z)
        def _():
            if at_z < last:

                @pl.loop(0, chunks // 2)
                def _(i):
                    carry_copy(1, 2 * i + x).wait_recv()
                    share_copy(2 * i + x).start()

            @pl.loop(0, chunks)
            def _(c):
                swap_copy(1, c).wait_recv()
                if at_z < last:

                    @pl.when(c % 2 != x)
                    def _():
                        share_copy(c).wait_recv()

                if at_z > 0:

                    @pl.when(c % 2 == x)
                    def _():
                        total, late_tag = joined(1, c)
                        keep = jnp.where(tag(ein, (1, c)) == late_tag, 1.0, 0.0)
                        eout[1, c, :BODY, :] = (total + body(ein, (1, c)) * keep).astype(BF)
                        eout[1, c, BODY:, :] = jnp.broadcast_to(late_tag, (PAD, HEAD)).astype(BF)
                        carry_copy(1, c).start()

                got_one = jnp.where(tag(ein, (1, c)) == final, 1.0, 0.0)
                total = near_part(1, c, final) + body(ein, (1, c)) * got_one
                state[1, chunk_at(c), :] = total.astype(BF)

    def pair_copy(p):
        return rc(pair.at[0, :, span(p)], pair.at[1, :, span(p)], psem, p, mate)

    def heads_loop(begin, stop, step):
        @pl.loop(begin, stop)
        def _(h):
            step(h, pl.ds(pl.multiple_of(h * HEAD, HEAD), HEAD))

    def inside(h, at):
        fq = feature(q_ref[:, at].astype(F32)).astype(BF)
        fq_ref[:, at] = fq
        weight = dot(fq, fk_ref[:, at], 1, 1).astype(BF) * mask_ref[...]
        weight_ref[h] = weight
        attn_ref[:, at] = dot(weight, v_ref[:, at], 1, 0)

    def local(c):
        heads_loop(c * HC, (c + 1) * HC, inside)

    def finish_head(h):
        at = pl.ds(pl.multiple_of(h * HEAD, HEAD), HEAD)
        outer = dot(fq_ref[:, at], state[0, at, :], 1, 0)
        attn = attn_ref[:, at] + jnp.where(col_ref[...] == first, outer, 0.0)
        inv = lax.rsqrt(jnp.mean(attn * attn, axis=-1, keepdims=True) + EPS)
        attn_ref[:, at] = attn
        pair[0, :, at] = (attn * inv * gain_ref[:, at]).astype(BF)

    def finish(c):
        for i in range(HC):
            finish_head(c * HC + i)
            if isinstance(c, int):
                pair_copy(i).start()
        if not isinstance(c, int):
            pair_copy(c + 1).start()

    def rest_of_states():
        @pl.loop(1, chunks)
        def _(c):
            carry(c)
            finish(c)

        later.swap.start()

    def turn(block):
        @pl.loop(0, 2)
        def _(i):
            k = block.k + 2 * i
            turned[k, 0] = whole[k, :, mine_at].T
            turned[k, 1] = theirs[k].T

    def swapped(block):
        block.swap.wait_recv()
        block.theirs_side.start()
        block.theirs_core.start()

    def mine_here(block):
        block.mine_side.wait_recv()
        block.mine_core.start()

    def rest_here(block):
        block.rest_side.wait_recv()
        block.rest_core.start()

    def theirs_here(block):
        block.theirs_side.wait_recv()
        block.far_core.start()

    def lead_ready():
        for block in (early, more):
            theirs_here(block)
        for block in (early, more):
            block.theirs_core.wait_recv()
            block.mine_core.wait_recv()
            block.far_core.wait_recv()
        core_two.wait_recv()
        turn(early)

    def product(at, dest):
        k = jnp.int32(0)
        for b in range(2):
            k = k + (1 << b) * ((dest // (1 << b) + j // (1 << b)) % 2)
        value = dot(turned[k, 0], pair[0, :, at], 1, 0) + dot(turned[k, 1], pair[1, :, at], 1, 0)
        return value * factor

    def partial(p, dest):
        return product(span(p), dest)

    low = 1 - z // (depth // 2)

    def going(w, t):
        return z + (1 - 2 * w) * (last - t)

    def chain(w, p, dest, slot):
        return pltpu.make_async_remote_copy(
            src_ref=sent.at[dest, :, span(p)], dst_ref=got.at[slot, :, span(p)],
            send_sem=ssem.at[p * depth + dest], recv_sem=rsem.at[p * (depth + 1) + slot],
            device_id={"seq": lax.rem(me + 2 - 4 * w + n, n)}, device_id_type=MESH,
        )

    def slot_of(w, t):
        return going(w, t) * (1 - w) + depth * w if t == last - 1 else going(w, t)

    def on_way(w, t):
        return (z <= t) if w == 0 else (z >= last - t)

    def send_end(p, t):
        @pl.when(end)
        def _():
            w = 1 - low
            dest = going(w, t)
            sent[dest, :, span(p)] = partial(p, dest).astype(BF)
            chain(w, p, dest, slot_of(w, t)).start()

    def relay(p, w, t):
        @pl.when(inner)
        def _():
            dest = going(w, t)
            size = span(p).size
            acc[:, :size] = partial(p, dest)
            chain(w, p, dest, dest).wait_recv()
            sent[dest, :, span(p)] = (acc[:, :size] + got[dest, :, span(p)].astype(F32)).astype(BF)
            chain(w, p, dest, slot_of(w, t)).start()

    def onward(p, t):
        relay(p, 1 - low, t)

    def returning(p):
        relay(p, low, last - 1)

    def later_pieces(step, begin):
        @pl.loop(begin, pieces)
        def _(p):
            step(p)

    def paired(p, cond):
        @pl.when(cond)
        def _():
            pair_copy(p).wait_recv()

    def upstream(c):
        at = slice(c * BODY, (c + 1) * BODY)
        total = None
        for k in range(tp):
            owner = jnp.int32(0)
            for b in range(2):
                owner = owner + (1 << b) * (((k >> b) + j // (1 << b)) % 2)
            start = pl.multiple_of(owner * width, width)
            term = dot(whole[k], w_ref[at, pl.ds(start, width)], 1, 1)
            total = term if total is None else total + term
        left, right = [], []
        for i in range(HC):
            cut = slice(c * BODY + i * HEAD, c * BODY + (i + 1) * HEAD)
            attn = attn_ref[:, cut]
            inv = lax.rsqrt(jnp.mean(attn * attn, axis=-1, keepdims=True) + EPS)
            scaled = total[:, i * HEAD : (i + 1) * HEAD] * gain_ref[:, cut]
            mean = jnp.mean(attn * scaled, axis=-1, keepdims=True)
            grad = (scaled * inv - attn * (inv * inv * inv) * mean).astype(BF)
            grad_ref[:, cut] = grad
            left.append(jnp.where(col_ref[...] == first, fq_ref[:, cut].astype(F32), 0.0).astype(BF))
            right.append(grad)
        put(1, c, left, right, first)

    def inside_back(h, at):
        g = grad_ref[:, at]
        gw = dot(g, v_ref[:, at], 1, 1).astype(BF) * mask_ref[...]
        vp_ref[:, at] = dot(weight_ref[h], g, 0, 0)
        kp_ref[:, at] = dot(gw, fq_ref[:, at], 0, 0)
        outer = dot(g, state[0, at, :], 1, 1)
        qp = dot(gw, fk_ref[:, at], 1, 0) + jnp.where(col_ref[...] == first, outer, 0.0)
        oq_ref[:, at] = (qp * slope(q_ref[:, at].astype(F32))).astype(BF)

    def outside_back(h, at):
        late = col_ref[...] == final
        d = state[1, at, :]
        vp = vp_ref[:, at] + jnp.where(late, dot(fk_ref[:, at], d, 1, 0), 0.0)
        ov_ref[:, at] = vp.astype(BF)
        kp = kp_ref[:, at] + jnp.where(late, dot(v_ref[:, at], d, 1, 1), 0.0)
        ok_ref[:, at] = (kp * slope(k_ref[:, at].astype(F32))).astype(BF)

    def keys_put(c):
        ats = [slice((c * HC + i) * HEAD, (c * HC + i + 1) * HEAD) for i in range(HC)]
        picked = []
        for at in ats:
            fk = feature(k_ref[:, at].astype(F32))
            fk_ref[:, at] = fk.astype(BF)
            picked.append(jnp.where(col_ref[...] == final, fk, 0.0).astype(BF))
        put(0, c, picked, [v_ref[:, at] for at in ats], final)

    core_one.start()
    core_two.start()
    keys_put(0)

    @pl.when(lead == 0)
    def _():
        core_one.wait_recv()

    for block in (early, more):
        block.mine_side.start()
        block.swap.start()
    for c in range(1, chunks):
        keys_put(c)
    local(0)
    carry_at(0, 0)
    local(1)
    carry_at(1, 0)
    local(2)
    swapped(early)
    carry_at(2, 0)
    local(3)
    mine_here(early)
    mine_here(more)
    swapped(more)

    @pl.when(lead == 1)
    def _():
        core_one.wait_recv()

    later.mine_side.start()
    for block in (early, more, later):
        block.rest_side.start()
    carry_at(3, 0)
    finish(0)

    @pl.when(z < last)
    def _():
        rest_of_states()

    lead_ready()
    paired(0, end)
    send_end(0, 0)
    paired(1, end)
    send_end(1, 0)

    @pl.when(z == last)
    def _():
        rest_of_states()

    send_end(0, 2)
    send_end(1, 2)
    mine_here(later)
    paired(0, inner)
    onward(0, 1)
    paired(1, inner)
    onward(1, 1)
    paired(2, end)
    send_end(2, 0)
    paired(3, end)
    send_end(3, 0)
    load_w.wait()
    for block in (early, more, later):
        rest_here(block)
    for block in (early, more, later):
        block.rest_core.wait_recv()
    later.mine_core.wait_recv()
    upstream(0)
    paired(4, end)
    send_end(4, 0)
    paired(2, inner)
    onward(2, 1)
    upstream(1)
    paired(3, inner)
    onward(3, 1)
    swapped(later)
    send_end(2, 2)
    upstream(2)
    send_end(3, 2)
    paired(4, inner)
    onward(4, 1)
    theirs_here(later)
    later.theirs_core.wait_recv()
    later.far_core.wait_recv()
    turn(later)
    send_end(0, 1)
    send_end(1, 1)
    upstream(3)
    back(last)
    later_pieces(lambda p: send_end(p, 1), 2)
    send_end(4, 2)
    returning(0)
    returning(1)
    later_pieces(returning, 2)
    heads_loop(0, 2 * HC, inside_back)
    onward(0, 2)
    onward(1, 2)
    back(last - 1)
    heads_loop(2 * HC, 3 * HC, inside_back)
    onward(2, 2)
    heads_loop(3 * HC, 4 * HC, inside_back)
    back(last - 2)
    onward(3, 2)

    @pl.loop(0, chunks)
    def _(c):
        at = chunk_at(c)
        ow_ref[:, at] = product(at, z)

    back(0)
    onward(4, 2)
    heads_loop(0, chunks * HC, outside_back)
    for p in range(pieces):
        for w in range(2):

            @pl.when((z > 0) if w == 0 else (z < last))
            def _():
                slot = z if w == 0 else depth
                chain(w, p, z, slot).wait_recv()
                ow_ref[:, span(p)] += got[slot, :, span(p)].astype(F32)

    for copy in [core_one, core_two] + early.all + more.all + later.all:
        copy.wait_send()
    for c in range(chunks):
        swap_copy(0, c).wait_send()
        swap_copy(1, c).wait_send()

        @pl.when(z < last)
        def _():
            carry_copy(0, c).wait_send()

        @pl.when((z > 0) & (x == c % 2))
        def _():
            carry_copy(1, c).wait_send()

        @pl.when((z < last) & (x == c % 2))
        def _():
            share_copy(c).wait_send()

    for p in range(pieces):
        pair_copy(p).wait_send()
        for w in range(2):
            for t in range(last):

                @pl.when(on_way(w, t))
                def _():
                    chain(w, p, going(w, t), slot_of(w, t)).wait_send()


def local_kernel(queries, keys, values, grad_out, out_weight, norm_gain, doc_ids):
    rows, feats = queries.shape
    n = lax.axis_size("seq")
    tp = lax.axis_size("tp")
    depth = n // 2
    model = out_weight.shape[1]
    width = model // tp
    mrows = model // n
    chunks = feats // BODY
    heads = feats // HEAD
    dims = (n, tp, depth, mrows, width, 1.0 / math.sqrt(rows * n))
    vmem = pl.BlockSpec(memory_space=pltpu.VMEM)
    anyspace = pl.BlockSpec(memory_space=pl.ANY)
    wide = jax.ShapeDtypeStruct((rows, feats), BF)
    summed = pltpu.VMEM((2, chunks, BODY + PAD, HEAD), BF)
    sem = pltpu.SemaphoreType.DMA
    flops = 2 * rows * model * feats * 3
    return pl.pallas_call(
        functools.partial(layer_kernel, dims),
        in_specs=[vmem] * 3 + [anyspace] * 2 + [vmem] * 2,
        out_specs=[vmem] * 4,
        out_shape=[wide] * 3 + [jax.ShapeDtypeStruct((mrows, feats), F32)],
        scratch_shapes=[
            pltpu.VMEM((tp, rows, width), BF),
            pltpu.VMEM((tp, rows, mrows), BF),
            pltpu.VMEM((tp, 2, mrows, rows), BF),
            pltpu.VMEM((feats, model), BF),
            pltpu.VMEM((rows, feats), F32),
            pltpu.VMEM((rows, feats), BF),
            pltpu.VMEM((rows, feats), BF),
            pltpu.VMEM((heads, rows, rows), BF),
            pltpu.VMEM((rows, rows), BF),
            pltpu.VMEM((rows, HEAD), F32),
            pltpu.VMEM((2, rows, feats), BF),
            pltpu.VMEM((rows, feats), BF),
            pltpu.VMEM((rows, feats), F32),
            pltpu.VMEM((rows, feats), F32),
            pltpu.VMEM((2, feats, HEAD), BF),
            summed, summed, summed, summed,
            pltpu.VMEM((mrows, BODY), F32),
            pltpu.VMEM((depth, mrows, feats), BF),
            pltpu.VMEM((depth + 1, mrows, feats), BF),
            sem((2,)),
            sem((2, 26)),
            sem((2, chunks + 1)),
            sem((2, 2 * chunks)),
            sem((2, 2 * chunks)),
            sem((2, chunks)),
            sem(((chunks + 1) * depth,)),
            sem(((chunks + 1) * (depth + 1),)),
        ],
        compiler_params=pltpu.CompilerParams(
            collective_id=0, has_side_effects=True, vmem_limit_bytes=60 * 1024 * 1024
        ),
        cost_estimate=pl.CostEstimate(flops=flops, bytes_accessed=flops // 512, transcendentals=0),
        name="layer",
    )(queries, keys, values, grad_out, out_weight, norm_gain[None, :], doc_ids[None, :])


def local_general(queries, keys, values, grad_out, out_weight, norm_gain, doc_ids):
    rows, feats = queries.shape
    n = lax.axis_size("seq")
    me = lax.axis_index("seq")
    heads = feats // HEAD

    def split(array):
        return array.reshape(rows, heads, HEAD)

    def mul(spec, a, b):
        return jnp.einsum(spec, a, b, preferred_element_type=F32)

    q, k = split(queries.astype(F32)), split(keys.astype(F32))
    v, gain = split(values), norm_gain.reshape(heads, HEAD)
    fq, fk = feature(q).astype(BF), feature(k).astype(BF)
    first, final = doc_ids[0], doc_ids[-1]
    early, late = (doc_ids == first)[:, None, None], (doc_ids == final)[:, None, None]
    firsts, finals = lax.all_gather(first, "seq"), lax.all_gather(final, "seq")
    before = (jnp.arange(n) < me) & (finals == first)
    after = (jnp.arange(n) > me) & (firsts == final)

    def over(summary, chosen):
        whole = lax.all_gather(summary, "seq")
        return jnp.sum(jnp.where(chosen[:, None, None, None], whole, 0.0), axis=0).astype(BF)

    at = jnp.arange(rows)
    mask = (at[:, None] >= at[None, :]) & (doc_ids[:, None] == doc_ids[None, :])
    weight = jnp.where(mask, mul("thd,shd->hts", fq, fk), 0.0).astype(BF)
    state = over(mul("shd,she->hde", jnp.where(late, fk, 0), v), before)
    attn = mul("hts,she->the", weight, v)
    attn = attn + jnp.where(early, mul("thd,hde->the", fq, state), 0.0)
    inv = lax.rsqrt(jnp.mean(attn * attn, axis=-1, keepdims=True) + EPS)
    normed = (attn * inv * gain).astype(BF).reshape(rows, feats)
    go = lax.all_gather(grad_out, "tp", axis=1, tiled=True)
    share = mul("tm,tf->mf", go, normed) * (1.0 / math.sqrt(rows * n))
    proj = lax.psum_scatter(share, "seq", scatter_dimension=0, tiled=True)
    scaled = split(mul("tm,fm->tf", go, out_weight)) * gain
    mean = jnp.mean(attn * scaled, axis=-1, keepdims=True)
    grad = (scaled * inv - attn * inv**3 * mean).astype(BF)
    dstate = over(mul("thd,the->hde", jnp.where(early, fq, 0), grad), after)
    gw = jnp.where(mask, mul("the,she->hts", grad, v), 0.0).astype(BF)
    vp = mul("hts,the->she", weight, grad) + jnp.where(late, mul("shd,hde->she", fk, dstate), 0.0)
    kp = mul("hts,thd->shd", gw, fq) + jnp.where(late, mul("she,hde->shd", v, dstate), 0.0)
    qp = mul("hts,shd->thd", gw, fk) + jnp.where(early, mul("the,hde->thd", grad, state), 0.0)
    outs = [qp * slope(q), kp * slope(k), vp]
    return tuple(o.astype(BF).reshape(rows, feats) for o in outs) + (proj,)


def solution(mesh):
    wide = P("seq", "tp")
    in_specs = (wide, wide, wide, wide, P("tp", None), P("tp"), P("seq"))
    local = local_kernel if mesh.shape["seq"] == 8 and mesh.shape["tp"] == 4 else local_general
    return jax.shard_map(
        local, mesh=mesh, in_specs=in_specs, out_specs=(wide,) * 4, check_vma=False
    )
```

```python
import functools
import math

import jax
import jax.numpy as jnp
from jax import lax
from jax.experimental import pallas as pl
from jax.experimental.pallas import tpu as pltpu
from jax.sharding import PartitionSpec as P

HEAD = 128
EPS = 1e-06
PAD = 16
HC = 2
BODY = HC * HEAD
BF = jnp.bfloat16
F32 = jnp.float32
MESH = pl.DeviceIdType.MESH


def feature(x):
    return jnp.where(x > 0, x + 1.0, jnp.exp(jnp.minimum(x, 0.0)))


def slope(x):
    return jnp.where(x > 0, 1.0, jnp.exp(jnp.minimum(x, 0.0)))


def dot(a, b, ca, cb):
    return lax.dot_general(a, b, (((ca,), (cb,)), ((), ())), preferred_element_type=F32)


def layer_kernel(
    dims, q_ref, k_ref, v_ref, go_hbm, w_hbm, gain_ref, doc_ref,
    oq_ref, ok_ref, ov_ref, ow_ref,
    whole, theirs, turned, w_ref, attn_ref, fq_ref, fk_ref, weight_ref, mask_ref, col_ref,
    pair, grad_ref, vp_ref, kp_ref, state, own, oth, ein, eout, acc, sent, got,
    lsem, gsem, psem, osem, esem, hsem, ssem, rsem,
):
    n, tp, depth, mrows, width, factor = dims
    rows, feats = q_ref.shape
    chunks = feats // BODY
    pieces = chunks + 1

    def span(p):
        if isinstance(p, int) and p < 2:
            return pl.ds(p * HEAD, HEAD)
        return pl.ds(pl.multiple_of((p - 1) * BODY, BODY), BODY)

    me = lax.axis_index("seq")
    j = lax.axis_index("tp")
    x = me % 2
    z = me // 2
    last = depth - 1
    mate = {"seq": me + 1 - 2 * x}
    core = {"tp": j + 1 - 2 * (j % 2)}
    side = {"tp": j + 2 - 4 * (j // 2)}
    odd = j % 2
    lead = odd * (1 - z // (depth // 2)) + (1 - odd) * (z // (depth // 2))
    end = (z == 0) | (z == last)
    inner = (z > 0) & (z < last)
    mine_at = pl.ds(pl.multiple_of(x * mrows, mrows), mrows)
    mate_at = pl.ds(pl.multiple_of((1 - x) * mrows, mrows), mrows)

    def rc(src, dst, sems, at, dev):
        return pltpu.make_async_remote_copy(
            src_ref=src, dst_ref=dst, send_sem=sems.at[0, at], recv_sem=sems.at[1, at],
            device_id=dev, device_id_type=MESH,
        )

    load_go = pltpu.make_async_copy(go_hbm, whole.at[0], lsem.at[0])
    load_w = pltpu.make_async_copy(w_hbm, w_ref, lsem.at[1])
    load_go.start()
    load_w.start()

    barrier = pltpu.get_barrier_semaphore()
    fixed = [mate, core, side]
    for dev in fixed:
        pl.semaphore_signal(barrier, inc=1, device_id=dev, device_id_type=MESH)

    @pl.when(z > 0)
    def _():
        pl.semaphore_signal(barrier, inc=1, device_id={"seq": me - 2}, device_id_type=MESH)

    @pl.when(z < last)
    def _():
        pl.semaphore_signal(barrier, inc=1, device_id={"seq": me + 2}, device_id_type=MESH)

    row = doc_ref[...].astype(F32)
    first = row[:, 0:1]
    final = row[:, rows - 1 : rows]
    col_ref[...] = jnp.broadcast_to(row, (HEAD, rows)).T
    for i in range(rows // HEAD):
        cut = slice(i * HEAD, (i + 1) * HEAD)
        at = lax.broadcasted_iota(jnp.int32, (rows, HEAD), 0)
        to = lax.broadcasted_iota(jnp.int32, (rows, HEAD), 1) + i * HEAD
        keep = (at >= to) & (col_ref[...] == row[:, cut])
        mask_ref[:, cut] = jnp.where(keep, 1.0, 0.0).astype(BF)

    sides = (z + depth - 1) // depth + (last - z + depth - 1) // depth
    pl.semaphore_wait(barrier, len(fixed) + sides)
    load_go.wait()

    half = rows // 2
    theirs_first = pl.ds(pl.multiple_of(lead * half, half), half)
    mine_first = pl.ds(pl.multiple_of((1 - lead) * half, half), half)
    core_one = rc(whole.at[0, theirs_first], whole.at[1, theirs_first], gsem, 24, core)
    core_two = rc(whole.at[0, mine_first], whole.at[1, mine_first], gsem, 25, core)

    class Block:
        def __init__(self, p, offset, size, slot):
            k = 1 - lead if p == 0 else lead
            part = pl.ds(pl.multiple_of((1 - lead) * half + offset, size), size)
            flip = 1 - k
            self.k = k
            names = ("swap", "mine_side", "rest_side", "theirs_side", "mine_core", "rest_core", "theirs_core", "far_core")
            ends = (
                (whole.at[k, part, mate_at], theirs.at[k, part], mate),
                (whole.at[k, part, mine_at], whole.at[k + 2, part, mine_at], side),
                (whole.at[k, part, mate_at], whole.at[k + 2, part, mate_at], side),
                (theirs.at[k, part], theirs.at[k + 2, part], side),
                (whole.at[k + 2, part, mine_at], whole.at[flip + 2, part, mine_at], core),
                (whole.at[k + 2, part, mate_at], whole.at[flip + 2, part, mate_at], core),
                (theirs.at[k, part], theirs.at[flip, part], core),
                (theirs.at[k + 2, part], theirs.at[flip + 2, part], core),
            )
            self.all = []
            for i, (name, (src, dst, dev)) in enumerate(zip(names, ends)):
                copy = rc(src, dst, gsem, slot * 8 + i, dev)
                setattr(self, name, copy)
                self.all.append(copy)

    early, more, later = Block(0, 0, half // 2, 0), Block(0, half // 2, half // 2, 1), Block(1, 0, half, 2)

    def swap_copy(w, c):
        return rc(own.at[w, c], oth.at[w, c], osem, w * chunks + c, mate)

    def carry_copy(w, c):
        return rc(eout.at[w, c], ein.at[w, c], esem, w * chunks + c, {"seq": lax.rem(me + 2 - 4 * w + n, n)})

    def put(w, c, left, right_at, edge):
        for i in range(HC):
            own[w, c, i * HEAD : (i + 1) * HEAD, :] = dot(left[i], right_at[i], 0, 0).astype(BF)
        own[w, c, BODY:, :] = jnp.broadcast_to(edge, (PAD, HEAD)).astype(BF)
        swap_copy(w, c).start()

    def share_copy(c):
        return rc(ein.at[1, c], ein.at[1, c], hsem, c, mate)

    def tag(ref, at):
        return ref[at + (slice(BODY, BODY + 1), slice(None))].astype(F32)

    def body(ref, at):
        return ref[at + (slice(0, BODY), slice(None))].astype(F32)

    def joined(w, c):
        ta, tb = tag(own, (w, c)), tag(oth, (w, c))
        front = x == w
        late_tag = jnp.where(front, tb, ta)
        same = jnp.where(ta == tb, 1.0, 0.0)
        keep_a = jnp.where(front, same, 1.0)
        keep_b = jnp.where(front, 1.0, same)
        return body(own, (w, c)) * keep_a + body(oth, (w, c)) * keep_b, late_tag

    def chunk_at(c):
        return pl.ds(pl.multiple_of(c * BODY, BODY), BODY)

    def near_part(w, c, edge):
        near = jnp.where(x == w, 0.0, jnp.where(tag(oth, (w, c)) == edge, 1.0, 0.0))
        return body(oth, (w, c)) * near

    @pl.when(z == 0)
    def _():
        ein[0] = jnp.zeros(ein.shape[1:], BF)

    @pl.when(z == last)
    def _():
        ein[1] = jnp.zeros(ein.shape[1:], BF)

    def carry(c):
        swap_copy(0, c).wait_recv()

        @pl.when(z > 0)
        def _():
            carry_copy(0, c).wait_recv()

        @pl.when(z < last)
        def _():
            total, late_tag = joined(0, c)
            keep = jnp.where(tag(ein, (0, c)) == late_tag, 1.0, 0.0)
            eout[0, c, :BODY, :] = (total + body(ein, (0, c)) * keep).astype(BF)
            eout[0, c, BODY:, :] = jnp.broadcast_to(late_tag, (PAD, HEAD)).astype(BF)
            carry_copy(0, c).start()

        got_one = jnp.where(tag(ein, (0, c)) == first, 1.0, 0.0)
        total = near_part(0, c, first) + body(ein, (0, c)) * got_one
        state[0, chunk_at(c), :] = total.astype(BF)

    def carry_at(at_z, c):
        @pl.when(z == at_z)
        def _():
            carry(c)

    def back(at_z):
        @pl.when(z == at_z)
        def _():
            if at_z < last:

                @pl.loop(0, chunks // 2)
                def _(i):
                    carry_copy(1, 2 * i + x).wait_recv()
                    share_copy(2 * i + x).start()

            @pl.loop(0, chunks)
            def _(c):
                swap_copy(1, c).wait_recv()
                if at_z < last:

                    @pl.when(c % 2 != x)
                    def _():
                        share_copy(c).wait_recv()

                if at_z > 0:

                    @pl.when(c % 2 == x)
                    def _():
                        total, late_tag = joined(1, c)
                        keep = jnp.where(tag(ein, (1, c)) == late_tag, 1.0, 0.0)
                        eout[1, c, :BODY, :] = (total + body(ein, (1, c)) * keep).astype(BF)
                        eout[1, c, BODY:, :] = jnp.broadcast_to(late_tag, (PAD, HEAD)).astype(BF)
                        carry_copy(1, c).start()

                got_one = jnp.where(tag(ein, (1, c)) == final, 1.0, 0.0)
                total = near_part(1, c, final) + body(ein, (1, c)) * got_one
                state[1, chunk_at(c), :] = total.astype(BF)

    def pair_copy(p):
        return rc(pair.at[0, :, span(p)], pair.at[1, :, span(p)], psem, p, mate)

    def heads_loop(begin, stop, step):
        @pl.loop(begin, stop)
        def _(h):
            step(h, pl.ds(pl.multiple_of(h * HEAD, HEAD), HEAD))

    def inside(h, at):
        fq = feature(q_ref[:, at].astype(F32)).astype(BF)
        fq_ref[:, at] = fq
        weight = dot(fq, fk_ref[:, at], 1, 1).astype(BF) * mask_ref[...]
        weight_ref[h] = weight
        attn_ref[:, at] = dot(weight, v_ref[:, at], 1, 0)

    def local(c):
        heads_loop(c * HC, (c + 1) * HC, inside)

    def finish_head(h):
        at = pl.ds(pl.multiple_of(h * HEAD, HEAD), HEAD)
        outer = dot(fq_ref[:, at], state[0, at, :], 1, 0)
        attn = attn_ref[:, at] + jnp.where(col_ref[...] == first, outer, 0.0)
        inv = lax.rsqrt(jnp.mean(attn * attn, axis=-1, keepdims=True) + EPS)
        attn_ref[:, at] = attn
        pair[0, :, at] = (attn * inv * gain_ref[:, at]).astype(BF)

    def finish(c):
        for i in range(HC):
            finish_head(c * HC + i)
            if isinstance(c, int):
                pair_copy(i).start()
        if not isinstance(c, int):
            pair_copy(c + 1).start()

    def rest_of_states():
        @pl.loop(1, chunks - 1)
        def _(c):
            carry(c)
            finish(c)

        later.swap.start()
        carry(chunks - 1)
        finish(jnp.int32(chunks - 1))

    def turn(block):
        @pl.loop(0, 2)
        def _(i):
            k = block.k + 2 * i
            turned[k, 0] = whole[k, :, mine_at].T
            turned[k, 1] = theirs[k].T

    def swapped(block):
        block.swap.wait_recv()
        block.theirs_side.start()
        block.theirs_core.start()

    def mine_here(block):
        block.mine_side.wait_recv()
        block.mine_core.start()

    def rest_here(block):
        block.rest_side.wait_recv()
        block.rest_core.start()

    def theirs_here(block):
        block.theirs_side.wait_recv()
        block.far_core.start()

    def lead_ready():
        for block in (early, more):
            theirs_here(block)
        for block in (early, more):
            block.theirs_core.wait_recv()
            block.mine_core.wait_recv()
            block.far_core.wait_recv()
        core_two.wait_recv()
        turn(early)

    def product(at, dest):
        k = jnp.int32(0)
        for b in range(2):
            k = k + (1 << b) * ((dest // (1 << b) + j // (1 << b)) % 2)
        value = dot(turned[k, 0], pair[0, :, at], 1, 0) + dot(turned[k, 1], pair[1, :, at], 1, 0)
        return value * factor

    def partial(p, dest):
        return product(span(p), dest)

    low = 1 - z // (depth // 2)

    def going(w, t):
        return z + (1 - 2 * w) * (last - t)

    def chain(w, p, dest, slot):
        return pltpu.make_async_remote_copy(
            src_ref=sent.at[dest, :, span(p)], dst_ref=got.at[slot, :, span(p)],
            send_sem=ssem.at[p * depth + dest], recv_sem=rsem.at[p * (depth + 1) + slot],
            device_id={"seq": lax.rem(me + 2 - 4 * w + n, n)}, device_id_type=MESH,
        )

    def slot_of(w, t):
        return going(w, t) * (1 - w) + depth * w if t == last - 1 else going(w, t)

    def on_way(w, t):
        return (z <= t) if w == 0 else (z >= last - t)

    def send_end(p, t):
        @pl.when(end)
        def _():
            w = 1 - low
            dest = going(w, t)
            sent[dest, :, span(p)] = partial(p, dest).astype(BF)
            chain(w, p, dest, slot_of(w, t)).start()

    def relay(p, w, t):
        @pl.when(inner)
        def _():
            dest = going(w, t)
            size = span(p).size
            acc[:, :size] = partial(p, dest)
            chain(w, p, dest, dest).wait_recv()
            sent[dest, :, span(p)] = (acc[:, :size] + got[dest, :, span(p)].astype(F32)).astype(BF)
            chain(w, p, dest, slot_of(w, t)).start()

    def onward(p, t):
        relay(p, 1 - low, t)

    def returning(p):
        relay(p, low, last - 1)

    def later_pieces(step, begin):
        @pl.loop(begin, pieces)
        def _(p):
            step(p)

    def paired(p, cond):
        @pl.when(cond)
        def _():
            pair_copy(p).wait_recv()

    def upstream(c):
        at = slice(c * BODY, (c + 1) * BODY)
        total = None
        for k in range(tp):
            owner = jnp.int32(0)
            for b in range(2):
                owner = owner + (1 << b) * (((k >> b) + j // (1 << b)) % 2)
            start = pl.multiple_of(owner * width, width)
            term = dot(whole[k], w_ref[at, pl.ds(start, width)], 1, 1)
            total = term if total is None else total + term
        left, right = [], []
        for i in range(HC):
            cut = slice(c * BODY + i * HEAD, c * BODY + (i + 1) * HEAD)
            attn = attn_ref[:, cut]
            inv = lax.rsqrt(jnp.mean(attn * attn, axis=-1, keepdims=True) + EPS)
            scaled = total[:, i * HEAD : (i + 1) * HEAD] * gain_ref[:, cut]
            mean = jnp.mean(attn * scaled, axis=-1, keepdims=True)
            grad = (scaled * inv - attn * (inv * inv * inv) * mean).astype(BF)
            grad_ref[:, cut] = grad
            left.append(jnp.where(col_ref[...] == first, fq_ref[:, cut].astype(F32), 0.0).astype(BF))
            right.append(grad)
        put(1, c, left, right, first)

    def inside_back(h, at):
        g = grad_ref[:, at]
        gw = dot(g, v_ref[:, at], 1, 1).astype(BF) * mask_ref[...]
        vp_ref[:, at] = dot(weight_ref[h], g, 0, 0)
        kp_ref[:, at] = dot(gw, fq_ref[:, at], 0, 0)
        outer = dot(g, state[0, at, :], 1, 1)
        qp = dot(gw, fk_ref[:, at], 1, 0) + jnp.where(col_ref[...] == first, outer, 0.0)
        oq_ref[:, at] = (qp * slope(q_ref[:, at].astype(F32))).astype(BF)

    def outside_back(h, at):
        late = col_ref[...] == final
        d = state[1, at, :]
        vp = vp_ref[:, at] + jnp.where(late, dot(fk_ref[:, at], d, 1, 0), 0.0)
        ov_ref[:, at] = vp.astype(BF)
        kp = kp_ref[:, at] + jnp.where(late, dot(v_ref[:, at], d, 1, 1), 0.0)
        ok_ref[:, at] = (kp * slope(k_ref[:, at].astype(F32))).astype(BF)

    def keys_put(c):
        ats = [slice((c * HC + i) * HEAD, (c * HC + i + 1) * HEAD) for i in range(HC)]
        picked = []
        for at in ats:
            fk = feature(k_ref[:, at].astype(F32))
            fk_ref[:, at] = fk.astype(BF)
            picked.append(jnp.where(col_ref[...] == final, fk, 0.0).astype(BF))
        put(0, c, picked, [v_ref[:, at] for at in ats], final)

    core_one.start()
    core_two.start()
    keys_put(0)

    @pl.when(lead == 0)
    def _():
        core_one.wait_recv()

    for block in (early, more):
        block.mine_side.start()
        block.swap.start()
    for c in range(1, chunks):
        keys_put(c)
    local(0)
    carry_at(0, 0)
    local(1)
    carry_at(1, 0)
    local(2)
    swapped(early)
    carry_at(2, 0)
    local(3)
    mine_here(early)
    mine_here(more)
    swapped(more)

    @pl.when(lead == 1)
    def _():
        core_one.wait_recv()

    later.mine_side.start()
    for block in (early, more, later):
        block.rest_side.start()
    carry_at(3, 0)
    finish(0)

    @pl.when(z < last)
    def _():
        rest_of_states()

    lead_ready()
    paired(0, end)
    send_end(0, 0)
    paired(1, end)
    send_end(1, 0)

    @pl.when(z == last)
    def _():
        rest_of_states()

    send_end(0, 2)
    send_end(1, 2)
    mine_here(later)
    paired(0, inner)
    onward(0, 1)
    paired(1, inner)
    onward(1, 1)
    paired(2, end)
    send_end(2, 0)
    paired(3, end)
    send_end(3, 0)
    load_w.wait()
    for block in (early, more, later):
        rest_here(block)
    for block in (early, more, later):
        block.rest_core.wait_recv()
    later.mine_core.wait_recv()
    upstream(0)
    send_end(2, 2)
    paired(2, inner)
    onward(2, 1)
    swapped(later)
    upstream(1)
    paired(4, end)
    send_end(4, 0)
    paired(3, inner)
    onward(3, 1)
    theirs_here(later)
    later.theirs_core.wait_recv()
    later.far_core.wait_recv()
    turn(later)
    send_end(0, 1)
    send_end(1, 1)
    upstream(2)
    paired(4, inner)
    onward(4, 1)
    upstream(3)
    back(last)
    later_pieces(lambda p: send_end(p, 1), 2)
    send_end(3, 2)
    send_end(4, 2)
    returning(0)
    returning(1)
    later_pieces(returning, 2)
    heads_loop(0, 2 * HC, inside_back)
    onward(0, 2)
    onward(1, 2)
    back(last - 1)
    heads_loop(2 * HC, 3 * HC, inside_back)
    onward(2, 2)
    heads_loop(3 * HC, 4 * HC, inside_back)
    back(last - 2)
    onward(3, 2)

    @pl.loop(0, chunks)
    def _(c):
        at = chunk_at(c)
        ow_ref[:, at] = product(at, z)

    back(0)
    onward(4, 2)
    heads_loop(0, chunks * HC, outside_back)
    for p in range(pieces):
        for w in range(2):

            @pl.when((z > 0) if w == 0 else (z < last))
            def _():
                slot = z if w == 0 else depth
                chain(w, p, z, slot).wait_recv()
                ow_ref[:, span(p)] += got[slot, :, span(p)].astype(F32)

    for copy in [core_one, core_two] + early.all + more.all + later.all:
        copy.wait_send()
    for c in range(chunks):
        swap_copy(0, c).wait_send()
        swap_copy(1, c).wait_send()

        @pl.when(z < last)
        def _():
            carry_copy(0, c).wait_send()

        @pl.when((z > 0) & (x == c % 2))
        def _():
            carry_copy(1, c).wait_send()

        @pl.when((z < last) & (x == c % 2))
        def _():
            share_copy(c).wait_send()

    for p in range(pieces):
        pair_copy(p).wait_send()
        for w in range(2):
            for t in range(last):

                @pl.when(on_way(w, t))
                def _():
                    chain(w, p, going(w, t), slot_of(w, t)).wait_send()


def store_kernel(*refs):
    count = (len(refs) - 1) // 2
    sems = refs[-1]
    copies = []
    for i in range(count):
        rows = refs[i].shape[0] // 4
        for r in range(4):
            at = pl.ds(r * rows, rows)
            copies.append(pltpu.make_async_copy(refs[i].at[at], refs[count + i].at[at], sems.at[i, r]))
    for copy in copies:
        copy.start()
    for copy in copies:
        copy.wait()


def local_kernel(queries, keys, values, grad_out, out_weight, norm_gain, doc_ids):
    rows, feats = queries.shape
    n = lax.axis_size("seq")
    tp = lax.axis_size("tp")
    depth = n // 2
    model = out_weight.shape[1]
    width = model // tp
    mrows = model // n
    chunks = feats // BODY
    heads = feats // HEAD
    dims = (n, tp, depth, mrows, width, 1.0 / math.sqrt(rows * n))
    vmem = pl.BlockSpec(memory_space=pltpu.VMEM)
    anyspace = pl.BlockSpec(memory_space=pl.ANY)
    wide = jax.ShapeDtypeStruct((rows, feats), BF)
    summed = pltpu.VMEM((2, chunks, BODY + PAD, HEAD), BF)
    sem = pltpu.SemaphoreType.DMA
    flops = 2 * rows * model * feats * 3
    parts = pl.pallas_call(
        functools.partial(layer_kernel, dims),
        in_specs=[vmem] * 3 + [anyspace] * 2 + [vmem] * 2,
        out_specs=[vmem] * 4,
        out_shape=[pltpu.VMEM((rows, feats), BF)] * 3 + [pltpu.VMEM((mrows, feats), F32)],
        scratch_shapes=[
            pltpu.VMEM((tp, rows, width), BF),
            pltpu.VMEM((tp, rows, mrows), BF),
            pltpu.VMEM((tp, 2, mrows, rows), BF),
            pltpu.VMEM((feats, model), BF),
            pltpu.VMEM((rows, feats), F32),
            pltpu.VMEM((rows, feats), BF),
            pltpu.VMEM((rows, feats), BF),
            pltpu.VMEM((heads, rows, rows), BF),
            pltpu.VMEM((rows, rows), BF),
            pltpu.VMEM((rows, HEAD), F32),
            pltpu.VMEM((2, rows, feats), BF),
            pltpu.VMEM((rows, feats), BF),
            pltpu.VMEM((rows, feats), F32),
            pltpu.VMEM((rows, feats), F32),
            pltpu.VMEM((2, feats, HEAD), BF),
            summed, summed, summed, summed,
            pltpu.VMEM((mrows, BODY), F32),
            pltpu.VMEM((depth, mrows, feats), BF),
            pltpu.VMEM((depth + 1, mrows, feats), BF),
            sem((2,)),
            sem((2, 26)),
            sem((2, chunks + 1)),
            sem((2, 2 * chunks)),
            sem((2, 2 * chunks)),
            sem((2, chunks)),
            sem(((chunks + 1) * depth,)),
            sem(((chunks + 1) * (depth + 1),)),
        ],
        compiler_params=pltpu.CompilerParams(
            collective_id=0, has_side_effects=True, vmem_limit_bytes=52 * 1024 * 1024
        ),
        cost_estimate=pl.CostEstimate(flops=flops, bytes_accessed=flops // 512, transcendentals=0),
        name="layer",
    )(queries, keys, values, grad_out, out_weight, norm_gain[None, :], doc_ids[None, :])
    return pl.pallas_call(
        store_kernel,
        in_specs=[vmem] * 4,
        out_specs=[anyspace] * 4,
        out_shape=[wide] * 3 + [jax.ShapeDtypeStruct((mrows, feats), F32)],
        scratch_shapes=[sem((4, 4))],
        compiler_params=pltpu.CompilerParams(vmem_limit_bytes=1024 * 1024),
        name="store",
    )(*parts)


def local_general(queries, keys, values, grad_out, out_weight, norm_gain, doc_ids):
    rows, feats = queries.shape
    n = lax.axis_size("seq")
    me = lax.axis_index("seq")
    heads = feats // HEAD

    def split(array):
        return array.reshape(rows, heads, HEAD)

    def mul(spec, a, b):
        return jnp.einsum(spec, a, b, preferred_element_type=F32)

    q, k = split(queries.astype(F32)), split(keys.astype(F32))
    v, gain = split(values), norm_gain.reshape(heads, HEAD)
    fq, fk = feature(q).astype(BF), feature(k).astype(BF)
    first, final = doc_ids[0], doc_ids[-1]
    early, late = (doc_ids == first)[:, None, None], (doc_ids == final)[:, None, None]
    firsts, finals = lax.all_gather(first, "seq"), lax.all_gather(final, "seq")
    before = (jnp.arange(n) < me) & (finals == first)
    after = (jnp.arange(n) > me) & (firsts == final)

    def over(summary, chosen):
        whole = lax.all_gather(summary, "seq")
        return jnp.sum(jnp.where(chosen[:, None, None, None], whole, 0.0), axis=0).astype(BF)

    at = jnp.arange(rows)
    mask = (at[:, None] >= at[None, :]) & (doc_ids[:, None] == doc_ids[None, :])
    weight = jnp.where(mask, mul("thd,shd->hts", fq, fk), 0.0).astype(BF)
    state = over(mul("shd,she->hde", jnp.where(late, fk, 0), v), before)
    attn = mul("hts,she->the", weight, v)
    attn = attn + jnp.where(early, mul("thd,hde->the", fq, state), 0.0)
    inv = lax.rsqrt(jnp.mean(attn * attn, axis=-1, keepdims=True) + EPS)
    normed = (attn * inv * gain).astype(BF).reshape(rows, feats)
    go = lax.all_gather(grad_out, "tp", axis=1, tiled=True)
    share = mul("tm,tf->mf", go, normed) * (1.0 / math.sqrt(rows * n))
    proj = lax.psum_scatter(share, "seq", scatter_dimension=0, tiled=True)
    scaled = split(mul("tm,fm->tf", go, out_weight)) * gain
    mean = jnp.mean(attn * scaled, axis=-1, keepdims=True)
    grad = (scaled * inv - attn * inv**3 * mean).astype(BF)
    dstate = over(mul("thd,the->hde", jnp.where(early, fq, 0), grad), after)
    gw = jnp.where(mask, mul("the,she->hts", grad, v), 0.0).astype(BF)
    vp = mul("hts,the->she", weight, grad) + jnp.where(late, mul("shd,hde->she", fk, dstate), 0.0)
    kp = mul("hts,thd->shd", gw, fq) + jnp.where(late, mul("she,hde->shd", v, dstate), 0.0)
    qp = mul("hts,shd->thd", gw, fk) + jnp.where(early, mul("the,hde->thd", grad, state), 0.0)
    outs = [qp * slope(q), kp * slope(k), vp]
    return tuple(o.astype(BF).reshape(rows, feats) for o in outs) + (proj,)


def solution(mesh):
    wide = P("seq", "tp")
    in_specs = (wide, wide, wide, wide, P("tp", None), P("tp"), P("seq"))
    local = local_kernel if mesh.shape["seq"] == 8 and mesh.shape["tp"] == 4 else local_general
    return jax.shard_map(
        local, mesh=mesh, in_specs=in_specs, out_specs=(wide,) * 4, check_vma=False
    )
```

```python
import functools
import math

import jax
import jax.numpy as jnp
from jax import lax
from jax.experimental import pallas as pl
from jax.experimental.pallas import tpu as pltpu
from jax.sharding import PartitionSpec as P

HEAD = 128
EPS = 1e-06
PAD = 16
HC = 2
BODY = HC * HEAD
BF = jnp.bfloat16
F32 = jnp.float32
MESH = pl.DeviceIdType.MESH


def feature(x):
    return jnp.where(x > 0, x + 1.0, jnp.exp(jnp.minimum(x, 0.0)))


def slope(x):
    return jnp.where(x > 0, 1.0, jnp.exp(jnp.minimum(x, 0.0)))


def dot(a, b, ca, cb):
    return lax.dot_general(a, b, (((ca,), (cb,)), ((), ())), preferred_element_type=F32)


def layer_kernel(
    dims, q_hbm, k_hbm, v_hbm, go_hbm, w_hbm, gain_ref, doc_ref,
    oq_ref, ok_ref, ov_ref, ow_ref,
    q_ref, k_ref, v_ref, whole, theirs, turned, w_ref, attn_ref, fq_ref, fk_ref, weight_ref, mask_ref, col_ref,
    pair, grad_ref, vp_ref, kp_ref, state, own, oth, ein, eout, acc, sent, got,
    lsem, gsem, psem, osem, esem, hsem, ssem, rsem,
):
    n, tp, depth, mrows, width, factor = dims
    rows, feats = q_ref.shape
    chunks = feats // BODY
    pieces = chunks + 1

    def span(p):
        if isinstance(p, int) and p < 2:
            return pl.ds(p * HEAD, HEAD)
        return pl.ds(pl.multiple_of((p - 1) * BODY, BODY), BODY)

    me = lax.axis_index("seq")
    j = lax.axis_index("tp")
    x = me % 2
    z = me // 2
    last = depth - 1
    mate = {"seq": me + 1 - 2 * x}
    core = {"tp": j + 1 - 2 * (j % 2)}
    side = {"tp": j + 2 - 4 * (j // 2)}
    odd = j % 2
    lead = odd * (1 - z // (depth // 2)) + (1 - odd) * (z // (depth // 2))
    end = (z == 0) | (z == last)
    inner = (z > 0) & (z < last)
    mine_at = pl.ds(pl.multiple_of(x * mrows, mrows), mrows)
    mate_at = pl.ds(pl.multiple_of((1 - x) * mrows, mrows), mrows)

    def rc(src, dst, sems, at, dev):
        return pltpu.make_async_remote_copy(
            src_ref=src, dst_ref=dst, send_sem=sems.at[0, at], recv_sem=sems.at[1, at],
            device_id=dev, device_id_type=MESH,
        )

    load_go = pltpu.make_async_copy(go_hbm, whole.at[0], lsem.at[0])
    load_w = pltpu.make_async_copy(w_hbm, w_ref, lsem.at[1])
    load_k = pltpu.make_async_copy(k_hbm, k_ref, lsem.at[2])
    load_v = pltpu.make_async_copy(v_hbm, v_ref, lsem.at[3])
    load_q = pltpu.make_async_copy(q_hbm, q_ref, lsem.at[4])
    for load in (load_go, load_k, load_v, load_q):
        load.start()

    barrier = pltpu.get_barrier_semaphore()
    fixed = [mate, core, side]
    for dev in fixed:
        pl.semaphore_signal(barrier, inc=1, device_id=dev, device_id_type=MESH)

    @pl.when(z > 0)
    def _():
        pl.semaphore_signal(barrier, inc=1, device_id={"seq": me - 2}, device_id_type=MESH)

    @pl.when(z < last)
    def _():
        pl.semaphore_signal(barrier, inc=1, device_id={"seq": me + 2}, device_id_type=MESH)

    row = doc_ref[...].astype(F32)
    first = row[:, 0:1]
    final = row[:, rows - 1 : rows]
    col_ref[...] = jnp.broadcast_to(row, (HEAD, rows)).T
    for i in range(rows // HEAD):
        cut = slice(i * HEAD, (i + 1) * HEAD)
        at = lax.broadcasted_iota(jnp.int32, (rows, HEAD), 0)
        to = lax.broadcasted_iota(jnp.int32, (rows, HEAD), 1) + i * HEAD
        keep = (at >= to) & (col_ref[...] == row[:, cut])
        mask_ref[:, cut] = jnp.where(keep, 1.0, 0.0).astype(BF)

    sides = (z + depth - 1) // depth + (last - z + depth - 1) // depth
    pl.semaphore_wait(barrier, len(fixed) + sides)
    load_go.wait()

    half = rows // 2
    theirs_first = pl.ds(pl.multiple_of(lead * half, half), half)
    mine_first = pl.ds(pl.multiple_of((1 - lead) * half, half), half)
    core_one = rc(whole.at[0, theirs_first], whole.at[1, theirs_first], gsem, 24, core)
    core_two = rc(whole.at[0, mine_first], whole.at[1, mine_first], gsem, 25, core)

    class Block:
        def __init__(self, p, offset, size, slot):
            k = 1 - lead if p == 0 else lead
            part = pl.ds(pl.multiple_of((1 - lead) * half + offset, size), size)
            flip = 1 - k
            self.k = k
            names = ("swap", "mine_side", "rest_side", "theirs_side", "mine_core", "rest_core", "theirs_core", "far_core")
            ends = (
                (whole.at[k, part, mate_at], theirs.at[k, part], mate),
                (whole.at[k, part, mine_at], whole.at[k + 2, part, mine_at], side),
                (whole.at[k, part, mate_at], whole.at[k + 2, part, mate_at], side),
                (theirs.at[k, part], theirs.at[k + 2, part], side),
                (whole.at[k + 2, part, mine_at], whole.at[flip + 2, part, mine_at], core),
                (whole.at[k + 2, part, mate_at], whole.at[flip + 2, part, mate_at], core),
                (theirs.at[k, part], theirs.at[flip, part], core),
                (theirs.at[k + 2, part], theirs.at[flip + 2, part], core),
            )
            self.all = []
            for i, (name, (src, dst, dev)) in enumerate(zip(names, ends)):
                copy = rc(src, dst, gsem, slot * 8 + i, dev)
                setattr(self, name, copy)
                self.all.append(copy)

    early, more, later = Block(0, 0, half // 2, 0), Block(0, half // 2, half // 2, 1), Block(1, 0, half, 2)

    def swap_copy(w, c):
        return rc(own.at[w, c], oth.at[w, c], osem, w * chunks + c, mate)

    def carry_copy(w, c):
        return rc(eout.at[w, c], ein.at[w, c], esem, w * chunks + c, {"seq": lax.rem(me + 2 - 4 * w + n, n)})

    def put(w, c, left, right_at, edge):
        for i in range(HC):
            own[w, c, i * HEAD : (i + 1) * HEAD, :] = dot(left[i], right_at[i], 0, 0).astype(BF)
        own[w, c, BODY:, :] = jnp.broadcast_to(edge, (PAD, HEAD)).astype(BF)
        swap_copy(w, c).start()

    def share_copy(c):
        return rc(ein.at[1, c], ein.at[1, c], hsem, c, mate)

    def tag(ref, at):
        return ref[at + (slice(BODY, BODY + 1), slice(None))].astype(F32)

    def body(ref, at):
        return ref[at + (slice(0, BODY), slice(None))].astype(F32)

    def joined(w, c):
        ta, tb = tag(own, (w, c)), tag(oth, (w, c))
        front = x == w
        late_tag = jnp.where(front, tb, ta)
        same = jnp.where(ta == tb, 1.0, 0.0)
        keep_a = jnp.where(front, same, 1.0)
        keep_b = jnp.where(front, 1.0, same)
        return body(own, (w, c)) * keep_a + body(oth, (w, c)) * keep_b, late_tag

    def chunk_at(c):
        return pl.ds(pl.multiple_of(c * BODY, BODY), BODY)

    def near_part(w, c, edge):
        near = jnp.where(x == w, 0.0, jnp.where(tag(oth, (w, c)) == edge, 1.0, 0.0))
        return body(oth, (w, c)) * near

    @pl.when(z == 0)
    def _():
        ein[0] = jnp.zeros(ein.shape[1:], BF)

    @pl.when(z == last)
    def _():
        ein[1] = jnp.zeros(ein.shape[1:], BF)

    def carry(c):
        swap_copy(0, c).wait_recv()

        @pl.when(z > 0)
        def _():
            carry_copy(0, c).wait_recv()

        @pl.when(z < last)
        def _():
            total, late_tag = joined(0, c)
            keep = jnp.where(tag(ein, (0, c)) == late_tag, 1.0, 0.0)
            eout[0, c, :BODY, :] = (total + body(ein, (0, c)) * keep).astype(BF)
            eout[0, c, BODY:, :] = jnp.broadcast_to(late_tag, (PAD, HEAD)).astype(BF)
            carry_copy(0, c).start()

        got_one = jnp.where(tag(ein, (0, c)) == first, 1.0, 0.0)
        total = near_part(0, c, first) + body(ein, (0, c)) * got_one
        state[0, chunk_at(c), :] = total.astype(BF)

    def carry_at(at_z, c):
        @pl.when(z == at_z)
        def _():
            carry(c)

    def back(at_z):
        @pl.when(z == at_z)
        def _():
            @pl.loop(0, chunks // 2)
            def _(i):
                c = 2 * i + x
                swap_copy(1, c).wait_recv()
                if at_z < last:
                    carry_copy(1, c).wait_recv()
                if at_z > 0:
                    total, late_tag = joined(1, c)
                    keep = jnp.where(tag(ein, (1, c)) == late_tag, 1.0, 0.0)
                    eout[1, c, :BODY, :] = (total + body(ein, (1, c)) * keep).astype(BF)
                    eout[1, c, BODY:, :] = jnp.broadcast_to(late_tag, (PAD, HEAD)).astype(BF)
                    carry_copy(1, c).start()
                if at_z < last:
                    share_copy(c).start()

            @pl.loop(0, chunks)
            def _(c):
                @pl.when(c % 2 != x)
                def _():
                    swap_copy(1, c).wait_recv()
                    if at_z < last:
                        share_copy(c).wait_recv()

                got_one = jnp.where(tag(ein, (1, c)) == final, 1.0, 0.0)
                total = near_part(1, c, final) + body(ein, (1, c)) * got_one
                state[1, chunk_at(c), :] = total.astype(BF)

    def pair_copy(p):
        return rc(pair.at[0, :, span(p)], pair.at[1, :, span(p)], psem, p, mate)

    def heads_loop(begin, stop, step):
        @pl.loop(begin, stop)
        def _(h):
            step(h, pl.ds(pl.multiple_of(h * HEAD, HEAD), HEAD))

    def inside(h, at):
        fq = feature(q_ref[:, at].astype(F32)).astype(BF)
        fq_ref[:, at] = fq
        weight = dot(fq, fk_ref[:, at], 1, 1).astype(BF) * mask_ref[...]
        weight_ref[h] = weight
        attn_ref[:, at] = dot(weight, v_ref[:, at], 1, 0)

    def local(c):
        heads_loop(c * HC, (c + 1) * HC, inside)

    def finish_head(h):
        at = pl.ds(pl.multiple_of(h * HEAD, HEAD), HEAD)
        outer = dot(fq_ref[:, at], state[0, at, :], 1, 0)
        attn = attn_ref[:, at] + jnp.where(col_ref[...] == first, outer, 0.0)
        inv = lax.rsqrt(jnp.mean(attn * attn, axis=-1, keepdims=True) + EPS)
        attn_ref[:, at] = attn
        pair[0, :, at] = (attn * inv * gain_ref[:, at]).astype(BF)

    def finish(c):
        for i in range(HC):
            finish_head(c * HC + i)
            if isinstance(c, int):
                pair_copy(i).start()
        if not isinstance(c, int):
            pair_copy(c + 1).start()

    def rest_of_states():
        @pl.loop(1, chunks - 1)
        def _(c):
            carry(c)
            finish(c)

        later.swap.start()
        carry(chunks - 1)
        finish(jnp.int32(chunks - 1))

    def turn(block):
        @pl.loop(0, 2)
        def _(i):
            k = block.k + 2 * i
            turned[k, 0] = whole[k, :, mine_at].T
            turned[k, 1] = theirs[k].T

    def swapped(block):
        block.swap.wait_recv()
        block.theirs_side.start()
        block.theirs_core.start()

    def mine_here(block):
        block.mine_side.wait_recv()
        block.mine_core.start()

    def rest_here(block):
        block.rest_side.wait_recv()
        block.rest_core.start()

    def theirs_here(block):
        block.theirs_side.wait_recv()
        block.far_core.start()

    def lead_ready():
        for block in (early, more):
            theirs_here(block)
        for block in (early, more):
            block.theirs_core.wait_recv()
            block.mine_core.wait_recv()
            block.far_core.wait_recv()
        core_two.wait_recv()
        turn(early)

    def product(at, dest):
        k = jnp.int32(0)
        for b in range(2):
            k = k + (1 << b) * ((dest // (1 << b) + j // (1 << b)) % 2)
        value = dot(turned[k, 0], pair[0, :, at], 1, 0) + dot(turned[k, 1], pair[1, :, at], 1, 0)
        return value * factor

    def partial(p, dest):
        return product(span(p), dest)

    low = 1 - z // (depth // 2)

    def going(w, t):
        return z + (1 - 2 * w) * (last - t)

    def chain(w, p, dest, slot):
        return pltpu.make_async_remote_copy(
            src_ref=sent.at[dest, :, span(p)], dst_ref=got.at[slot, :, span(p)],
            send_sem=ssem.at[p * depth + dest], recv_sem=rsem.at[p * (depth + 1) + slot],
            device_id={"seq": lax.rem(me + 2 - 4 * w + n, n)}, device_id_type=MESH,
        )

    def slot_of(w, t):
        return going(w, t) * (1 - w) + depth * w if t == last - 1 else going(w, t)

    def on_way(w, t):
        return (z <= t) if w == 0 else (z >= last - t)

    def send_end(p, t):
        @pl.when(end)
        def _():
            w = 1 - low
            dest = going(w, t)
            sent[dest, :, span(p)] = partial(p, dest).astype(BF)
            chain(w, p, dest, slot_of(w, t)).start()

    def relay(p, w, t):
        @pl.when(inner)
        def _():
            dest = going(w, t)
            size = span(p).size
            acc[:, :size] = partial(p, dest)
            chain(w, p, dest, dest).wait_recv()
            sent[dest, :, span(p)] = (acc[:, :size] + got[dest, :, span(p)].astype(F32)).astype(BF)
            chain(w, p, dest, slot_of(w, t)).start()

    def onward(p, t):
        relay(p, 1 - low, t)

    def returning(p):
        relay(p, low, last - 1)

    def later_pieces(step, begin):
        @pl.loop(begin, pieces)
        def _(p):
            step(p)

    def paired(p, cond):
        @pl.when(cond)
        def _():
            pair_copy(p).wait_recv()

    def upstream(c):
        at = slice(c * BODY, (c + 1) * BODY)
        total = None
        for k in range(tp):
            owner = jnp.int32(0)
            for b in range(2):
                owner = owner + (1 << b) * (((k >> b) + j // (1 << b)) % 2)
            start = pl.multiple_of(owner * width, width)
            term = dot(whole[k], w_ref[at, pl.ds(start, width)], 1, 1)
            total = term if total is None else total + term
        left, right = [], []
        for i in range(HC):
            cut = slice(c * BODY + i * HEAD, c * BODY + (i + 1) * HEAD)
            attn = attn_ref[:, cut]
            inv = lax.rsqrt(jnp.mean(attn * attn, axis=-1, keepdims=True) + EPS)
            scaled = total[:, i * HEAD : (i + 1) * HEAD] * gain_ref[:, cut]
            mean = jnp.mean(attn * scaled, axis=-1, keepdims=True)
            grad = (scaled * inv - attn * (inv * inv * inv) * mean).astype(BF)
            grad_ref[:, cut] = grad
            left.append(jnp.where(col_ref[...] == first, fq_ref[:, cut].astype(F32), 0.0).astype(BF))
            right.append(grad)
        put(1, c, left, right, first)

    def inside_back(h, at):
        g = grad_ref[:, at]
        gw = dot(g, v_ref[:, at], 1, 1).astype(BF) * mask_ref[...]
        vp_ref[:, at] = dot(weight_ref[h], g, 0, 0)
        kp_ref[:, at] = dot(gw, fq_ref[:, at], 0, 0)
        outer = dot(g, state[0, at, :], 1, 1)
        qp = dot(gw, fk_ref[:, at], 1, 0) + jnp.where(col_ref[...] == first, outer, 0.0)
        oq_ref[:, at] = (qp * slope(q_ref[:, at].astype(F32))).astype(BF)

    def outside_back(h, at):
        late = col_ref[...] == final
        d = state[1, at, :]
        vp = vp_ref[:, at] + jnp.where(late, dot(fk_ref[:, at], d, 1, 0), 0.0)
        ov_ref[:, at] = vp.astype(BF)
        kp = kp_ref[:, at] + jnp.where(late, dot(v_ref[:, at], d, 1, 1), 0.0)
        ok_ref[:, at] = (kp * slope(k_ref[:, at].astype(F32))).astype(BF)

    def keys_put(c):
        ats = [slice((c * HC + i) * HEAD, (c * HC + i + 1) * HEAD) for i in range(HC)]
        picked = []
        for at in ats:
            fk = feature(k_ref[:, at].astype(F32))
            fk_ref[:, at] = fk.astype(BF)
            picked.append(jnp.where(col_ref[...] == final, fk, 0.0).astype(BF))
        put(0, c, picked, [v_ref[:, at] for at in ats], final)

    core_one.start()
    core_two.start()
    load_k.wait()
    load_v.wait()
    keys_put(0)

    @pl.when(lead == 0)
    def _():
        core_one.wait_recv()

    for block in (early, more):
        block.mine_side.start()
        block.swap.start()
    for c in range(1, chunks):
        keys_put(c)
    load_q.wait()
    load_w.start()
    local(0)
    carry_at(0, 0)
    local(1)
    carry_at(1, 0)
    local(2)
    swapped(early)
    carry_at(2, 0)
    local(3)
    mine_here(early)
    mine_here(more)
    swapped(more)

    @pl.when(lead == 1)
    def _():
        core_one.wait_recv()

    later.mine_side.start()
    for block in (early, more, later):
        block.rest_side.start()
    carry_at(3, 0)
    finish(0)

    @pl.when(z < last)
    def _():
        rest_of_states()

    lead_ready()
    paired(0, end)
    send_end(0, 0)
    paired(1, end)
    send_end(1, 0)

    @pl.when(z == last)
    def _():
        rest_of_states()

    send_end(0, 2)
    send_end(1, 2)
    mine_here(later)
    paired(0, inner)
    onward(0, 1)
    paired(1, inner)
    onward(1, 1)
    paired(2, end)
    send_end(2, 0)
    send_end(2, 2)
    paired(3, end)
    send_end(3, 0)
    load_w.wait()
    for block in (early, more, later):
        rest_here(block)
    for block in (early, more, later):
        block.rest_core.wait_recv()
    later.mine_core.wait_recv()
    upstream(0)
    paired(2, inner)
    onward(2, 1)
    swapped(later)
    upstream(1)
    paired(4, end)
    send_end(4, 0)
    paired(3, inner)
    onward(3, 1)
    theirs_here(later)
    later.theirs_core.wait_recv()
    later.far_core.wait_recv()
    turn(later)
    send_end(0, 1)
    send_end(1, 1)
    send_end(2, 1)
    upstream(2)
    paired(4, inner)
    onward(4, 1)
    upstream(3)
    back(last)
    later_pieces(lambda p: send_end(p, 1), 3)
    send_end(3, 2)
    send_end(4, 2)
    onward(0, 2)
    onward(1, 2)
    returning(0)
    returning(1)
    returning(2)
    heads_loop(0, HC, inside_back)
    returning(3)
    onward(2, 2)
    heads_loop(HC, 2 * HC, inside_back)
    back(last - 1)
    onward(3, 2)
    back(last - 2)
    returning(4)
    heads_loop(2 * HC, 3 * HC, inside_back)
    onward(4, 2)
    heads_loop(3 * HC, 4 * HC, inside_back)

    @pl.loop(0, chunks)
    def _(c):
        at = chunk_at(c)
        ow_ref[:, at] = product(at, z)

    back(0)
    heads_loop(0, chunks * HC, outside_back)
    for p in range(pieces):
        for w in range(2):

            @pl.when((z > 0) if w == 0 else (z < last))
            def _():
                slot = z if w == 0 else depth
                chain(w, p, z, slot).wait_recv()
                ow_ref[:, span(p)] += got[slot, :, span(p)].astype(F32)

    for copy in [core_one, core_two] + early.all + more.all + later.all:
        copy.wait_send()
    for c in range(chunks):
        swap_copy(0, c).wait_send()
        swap_copy(1, c).wait_send()

        @pl.when(z < last)
        def _():
            carry_copy(0, c).wait_send()

        @pl.when((z > 0) & (x == c % 2))
        def _():
            carry_copy(1, c).wait_send()

        @pl.when((z < last) & (x == c % 2))
        def _():
            share_copy(c).wait_send()

    for p in range(pieces):
        pair_copy(p).wait_send()
        for w in range(2):
            for t in range(last):

                @pl.when(on_way(w, t))
                def _():
                    chain(w, p, going(w, t), slot_of(w, t)).wait_send()


def store_kernel(*refs):
    count = (len(refs) - 1) // 2
    sems = refs[-1]
    copies = []
    for i in range(count):
        rows = refs[i].shape[0] // 4
        for r in range(4):
            at = pl.ds(r * rows, rows)
            copies.append(pltpu.make_async_copy(refs[i].at[at], refs[count + i].at[at], sems.at[i, r]))
    for copy in copies:
        copy.start()
    for copy in copies:
        copy.wait()


def local_kernel(queries, keys, values, grad_out, out_weight, norm_gain, doc_ids):
    rows, feats = queries.shape
    n = lax.axis_size("seq")
    tp = lax.axis_size("tp")
    depth = n // 2
    model = out_weight.shape[1]
    width = model // tp
    mrows = model // n
    chunks = feats // BODY
    heads = feats // HEAD
    dims = (n, tp, depth, mrows, width, 1.0 / math.sqrt(rows * n))
    vmem = pl.BlockSpec(memory_space=pltpu.VMEM)
    anyspace = pl.BlockSpec(memory_space=pl.ANY)
    wide = jax.ShapeDtypeStruct((rows, feats), BF)
    summed = pltpu.VMEM((2, chunks, BODY + PAD, HEAD), BF)
    sem = pltpu.SemaphoreType.DMA
    flops = 2 * rows * model * feats * 3
    parts = pl.pallas_call(
        functools.partial(layer_kernel, dims),
        in_specs=[anyspace] * 5 + [vmem] * 2,
        out_specs=[vmem] * 4,
        out_shape=[pltpu.VMEM((rows, feats), BF)] * 3 + [pltpu.VMEM((mrows, feats), F32)],
        scratch_shapes=[
            pltpu.VMEM((rows, feats), BF),
            pltpu.VMEM((rows, feats), BF),
            pltpu.VMEM((rows, feats), BF),
            pltpu.VMEM((tp, rows, width), BF),
            pltpu.VMEM((tp, rows, mrows), BF),
            pltpu.VMEM((tp, 2, mrows, rows), BF),
            pltpu.VMEM((feats, model), BF),
            pltpu.VMEM((rows, feats), F32),
            pltpu.VMEM((rows, feats), BF),
            pltpu.VMEM((rows, feats), BF),
            pltpu.VMEM((heads, rows, rows), BF),
            pltpu.VMEM((rows, rows), BF),
            pltpu.VMEM((rows, HEAD), F32),
            pltpu.VMEM((2, rows, feats), BF),
            pltpu.VMEM((rows, feats), BF),
            pltpu.VMEM((rows, feats), F32),
            pltpu.VMEM((rows, feats), F32),
            pltpu.VMEM((2, feats, HEAD), BF),
            summed, summed, summed, summed,
            pltpu.VMEM((mrows, BODY), F32),
            pltpu.VMEM((depth, mrows, feats), BF),
            pltpu.VMEM((depth + 1, mrows, feats), BF),
            sem((5,)),
            sem((2, 26)),
            sem((2, chunks + 1)),
            sem((2, 2 * chunks)),
            sem((2, 2 * chunks)),
            sem((2, chunks)),
            sem(((chunks + 1) * depth,)),
            sem(((chunks + 1) * (depth + 1),)),
        ],
        compiler_params=pltpu.CompilerParams(
            collective_id=0, has_side_effects=True, vmem_limit_bytes=52 * 1024 * 1024
        ),
        cost_estimate=pl.CostEstimate(flops=flops, bytes_accessed=flops // 512, transcendentals=0),
        name="layer",
    )(queries, keys, values, grad_out, out_weight, norm_gain[None, :], doc_ids[None, :])
    return pl.pallas_call(
        store_kernel,
        in_specs=[vmem] * 4,
        out_specs=[anyspace] * 4,
        out_shape=[wide] * 3 + [jax.ShapeDtypeStruct((mrows, feats), F32)],
        scratch_shapes=[sem((4, 4))],
        compiler_params=pltpu.CompilerParams(vmem_limit_bytes=1024 * 1024),
        name="store",
    )(*parts)


def local_general(queries, keys, values, grad_out, out_weight, norm_gain, doc_ids):
    rows, feats = queries.shape
    n = lax.axis_size("seq")
    me = lax.axis_index("seq")
    heads = feats // HEAD

    def split(array):
        return array.reshape(rows, heads, HEAD)

    def mul(spec, a, b):
        return jnp.einsum(spec, a, b, preferred_element_type=F32)

    q, k = split(queries.astype(F32)), split(keys.astype(F32))
    v, gain = split(values), norm_gain.reshape(heads, HEAD)
    fq, fk = feature(q).astype(BF), feature(k).astype(BF)
    first, final = doc_ids[0], doc_ids[-1]
    early, late = (doc_ids == first)[:, None, None], (doc_ids == final)[:, None, None]
    firsts, finals = lax.all_gather(first, "seq"), lax.all_gather(final, "seq")
    before = (jnp.arange(n) < me) & (finals == first)
    after = (jnp.arange(n) > me) & (firsts == final)

    def over(summary, chosen):
        whole = lax.all_gather(summary, "seq")
        return jnp.sum(jnp.where(chosen[:, None, None, None], whole, 0.0), axis=0).astype(BF)

    at = jnp.arange(rows)
    mask = (at[:, None] >= at[None, :]) & (doc_ids[:, None] == doc_ids[None, :])
    weight = jnp.where(mask, mul("thd,shd->hts", fq, fk), 0.0).astype(BF)
    state = over(mul("shd,she->hde", jnp.where(late, fk, 0), v), before)
    attn = mul("hts,she->the", weight, v)
    attn = attn + jnp.where(early, mul("thd,hde->the", fq, state), 0.0)
    inv = lax.rsqrt(jnp.mean(attn * attn, axis=-1, keepdims=True) + EPS)
    normed = (attn * inv * gain).astype(BF).reshape(rows, feats)
    go = lax.all_gather(grad_out, "tp", axis=1, tiled=True)
    share = mul("tm,tf->mf", go, normed) * (1.0 / math.sqrt(rows * n))
    proj = lax.psum_scatter(share, "seq", scatter_dimension=0, tiled=True)
    scaled = split(mul("tm,fm->tf", go, out_weight)) * gain
    mean = jnp.mean(attn * scaled, axis=-1, keepdims=True)
    grad = (scaled * inv - attn * inv**3 * mean).astype(BF)
    dstate = over(mul("thd,the->hde", jnp.where(early, fq, 0), grad), after)
    gw = jnp.where(mask, mul("the,she->hts", grad, v), 0.0).astype(BF)
    vp = mul("hts,the->she", weight, grad) + jnp.where(late, mul("shd,hde->she", fk, dstate), 0.0)
    kp = mul("hts,thd->shd", gw, fq) + jnp.where(late, mul("she,hde->shd", v, dstate), 0.0)
    qp = mul("hts,shd->thd", gw, fk) + jnp.where(early, mul("the,hde->thd", grad, state), 0.0)
    outs = [qp * slope(q), kp * slope(k), vp]
    return tuple(o.astype(BF).reshape(rows, feats) for o in outs) + (proj,)


def solution(mesh):
    wide = P("seq", "tp")
    in_specs = (wide, wide, wide, wide, P("tp", None), P("tp"), P("seq"))
    local = local_kernel if mesh.shape["seq"] == 8 and mesh.shape["tp"] == 4 else local_general
    return jax.shard_map(
        local, mesh=mesh, in_specs=in_specs, out_specs=(wide,) * 4, check_vma=False
    )
```

```python
import functools
import math

import jax
import jax.numpy as jnp
from jax import lax
from jax.experimental import pallas as pl
from jax.experimental.pallas import tpu as pltpu
from jax.sharding import PartitionSpec as P

HEAD = 128
EPS = 1e-06
PAD = 16
HC = 2
BODY = HC * HEAD
BF = jnp.bfloat16
F32 = jnp.float32
MESH = pl.DeviceIdType.MESH


def feature(x):
    return jnp.where(x > 0, x + 1.0, jnp.exp(jnp.minimum(x, 0.0)))


def slope(x):
    return jnp.where(x > 0, 1.0, jnp.exp(jnp.minimum(x, 0.0)))


def dot(a, b, ca, cb):
    return lax.dot_general(a, b, (((ca,), (cb,)), ((), ())), preferred_element_type=F32)


def layer_kernel(
    dims, q_hbm, k_hbm, v_hbm, go_hbm, w_hbm, gain_ref, doc_ref,
    oq_ref, ok_ref, ov_ref, ow_ref,
    q_ref, k_ref, v_ref, whole, theirs, turned, w_ref, attn_ref, fq_ref, fk_ref, weight_ref, mask_ref, col_ref,
    pair, grad_ref, vp_ref, kp_ref, state, own, oth, ein, eout, acc, sent, got,
    lsem, gsem, psem, osem, esem, hsem, ssem, rsem,
):
    n, tp, depth, mrows, width, factor = dims
    rows, feats = q_ref.shape
    chunks = feats // BODY
    pieces = chunks + 1

    def span(p):
        if isinstance(p, int) and p < 2:
            return pl.ds(p * HEAD, HEAD)
        return pl.ds(pl.multiple_of((p - 1) * BODY, BODY), BODY)

    me = lax.axis_index("seq")
    j = lax.axis_index("tp")
    x = me % 2
    z = me // 2
    last = depth - 1
    mate = {"seq": me + 1 - 2 * x}
    core = {"tp": j + 1 - 2 * (j % 2)}
    side = {"tp": j + 2 - 4 * (j // 2)}
    odd = j % 2
    lead = odd * (1 - z // (depth // 2)) + (1 - odd) * (z // (depth // 2))
    end = (z == 0) | (z == last)
    inner = (z > 0) & (z < last)
    mine_at = pl.ds(pl.multiple_of(x * mrows, mrows), mrows)
    mate_at = pl.ds(pl.multiple_of((1 - x) * mrows, mrows), mrows)

    def rc(src, dst, sems, at, dev):
        return pltpu.make_async_remote_copy(
            src_ref=src, dst_ref=dst, send_sem=sems.at[0, at], recv_sem=sems.at[1, at],
            device_id=dev, device_id_type=MESH,
        )

    load_go = pltpu.make_async_copy(go_hbm, whole.at[0], lsem.at[0])
    load_w = pltpu.make_async_copy(w_hbm, w_ref, lsem.at[1])
    load_k = pltpu.make_async_copy(k_hbm, k_ref, lsem.at[2])
    load_v = pltpu.make_async_copy(v_hbm, v_ref, lsem.at[3])
    load_q = pltpu.make_async_copy(q_hbm, q_ref, lsem.at[4])
    for load in (load_go, load_k, load_v, load_q):
        load.start()

    barrier = pltpu.get_barrier_semaphore()
    fixed = [mate, core, side]
    for dev in fixed:
        pl.semaphore_signal(barrier, inc=1, device_id=dev, device_id_type=MESH)

    @pl.when(z > 0)
    def _():
        pl.semaphore_signal(barrier, inc=1, device_id={"seq": me - 2}, device_id_type=MESH)

    @pl.when(z < last)
    def _():
        pl.semaphore_signal(barrier, inc=1, device_id={"seq": me + 2}, device_id_type=MESH)

    row = doc_ref[...].astype(F32)
    first = row[:, 0:1]
    final = row[:, rows - 1 : rows]
    col_ref[...] = jnp.broadcast_to(row, (HEAD, rows)).T
    for i in range(rows // HEAD):
        cut = slice(i * HEAD, (i + 1) * HEAD)
        at = lax.broadcasted_iota(jnp.int32, (rows, HEAD), 0)
        to = lax.broadcasted_iota(jnp.int32, (rows, HEAD), 1) + i * HEAD
        keep = (at >= to) & (col_ref[...] == row[:, cut])
        mask_ref[:, cut] = jnp.where(keep, 1.0, 0.0).astype(BF)

    sides = (z + depth - 1) // depth + (last - z + depth - 1) // depth
    pl.semaphore_wait(barrier, len(fixed) + sides)
    load_go.wait()

    half = rows // 2
    theirs_first = pl.ds(pl.multiple_of(lead * half, half), half)
    mine_first = pl.ds(pl.multiple_of((1 - lead) * half, half), half)
    core_one = rc(whole.at[0, theirs_first], whole.at[1, theirs_first], gsem, 24, core)
    core_two = rc(whole.at[0, mine_first], whole.at[1, mine_first], gsem, 25, core)

    class Block:
        def __init__(self, p, offset, size, slot):
            k = 1 - lead if p == 0 else lead
            part = pl.ds(pl.multiple_of((1 - lead) * half + offset, size), size)
            flip = 1 - k
            self.k = k
            names = ("swap", "mine_side", "rest_side", "theirs_side", "mine_core", "rest_core", "theirs_core", "far_core")
            ends = (
                (whole.at[k, part, mate_at], theirs.at[k, part], mate),
                (whole.at[k, part, mine_at], whole.at[k + 2, part, mine_at], side),
                (whole.at[k, part, mate_at], whole.at[k + 2, part, mate_at], side),
                (theirs.at[k, part], theirs.at[k + 2, part], side),
                (whole.at[k + 2, part, mine_at], whole.at[flip + 2, part, mine_at], core),
                (whole.at[k + 2, part, mate_at], whole.at[flip + 2, part, mate_at], core),
                (theirs.at[k, part], theirs.at[flip, part], core),
                (theirs.at[k + 2, part], theirs.at[flip + 2, part], core),
            )
            self.all = []
            for i, (name, (src, dst, dev)) in enumerate(zip(names, ends)):
                copy = rc(src, dst, gsem, slot * 8 + i, dev)
                setattr(self, name, copy)
                self.all.append(copy)

    early, more, later = Block(0, 0, half // 2, 0), Block(0, half // 2, half // 2, 1), Block(1, 0, half, 2)

    def swap_copy(w, c):
        return rc(own.at[w, c], oth.at[w, c], osem, w * chunks + c, mate)

    def carry_copy(w, c):
        return rc(eout.at[w, c], ein.at[w, c], esem, w * chunks + c, {"seq": lax.rem(me + 2 - 4 * w + n, n)})

    def put(w, c, left, right_at, edge):
        for i in range(HC):
            own[w, c, i * HEAD : (i + 1) * HEAD, :] = dot(left[i], right_at[i], 0, 0).astype(BF)
        own[w, c, BODY:, :] = jnp.broadcast_to(edge, (PAD, HEAD)).astype(BF)
        swap_copy(w, c).start()

    def share_copy(c):
        return rc(ein.at[1, c], ein.at[1, c], hsem, c, mate)

    def tag(ref, at):
        return ref[at + (slice(BODY, BODY + 1), slice(None))].astype(F32)

    def body(ref, at):
        return ref[at + (slice(0, BODY), slice(None))].astype(F32)

    def joined(w, c):
        ta, tb = tag(own, (w, c)), tag(oth, (w, c))
        front = x == w
        late_tag = jnp.where(front, tb, ta)
        same = jnp.where(ta == tb, 1.0, 0.0)
        keep_a = jnp.where(front, same, 1.0)
        keep_b = jnp.where(front, 1.0, same)
        return body(own, (w, c)) * keep_a + body(oth, (w, c)) * keep_b, late_tag

    def chunk_at(c):
        return pl.ds(pl.multiple_of(c * BODY, BODY), BODY)

    def near_part(w, c, edge):
        near = jnp.where(x == w, 0.0, jnp.where(tag(oth, (w, c)) == edge, 1.0, 0.0))
        return body(oth, (w, c)) * near

    @pl.when(z == 0)
    def _():
        ein[0] = jnp.zeros(ein.shape[1:], BF)

    @pl.when(z == last)
    def _():
        ein[1] = jnp.zeros(ein.shape[1:], BF)

    def carry(c):
        swap_copy(0, c).wait_recv()

        @pl.when(z > 0)
        def _():
            carry_copy(0, c).wait_recv()

        @pl.when(z < last)
        def _():
            total, late_tag = joined(0, c)
            keep = jnp.where(tag(ein, (0, c)) == late_tag, 1.0, 0.0)
            eout[0, c, :BODY, :] = (total + body(ein, (0, c)) * keep).astype(BF)
            eout[0, c, BODY:, :] = jnp.broadcast_to(late_tag, (PAD, HEAD)).astype(BF)
            carry_copy(0, c).start()

        got_one = jnp.where(tag(ein, (0, c)) == first, 1.0, 0.0)
        total = near_part(0, c, first) + body(ein, (0, c)) * got_one
        state[0, chunk_at(c), :] = total.astype(BF)

    def carry_at(at_z, c):
        @pl.when(z == at_z)
        def _():
            carry(c)
            finish(c)

    def back(at_z):
        @pl.when(z == at_z)
        def _():
            @pl.loop(0, chunks // 2)
            def _(i):
                c = 2 * i + x
                swap_copy(1, c).wait_recv()
                if at_z < last:
                    carry_copy(1, c).wait_recv()
                if at_z > 0:
                    total, late_tag = joined(1, c)
                    keep = jnp.where(tag(ein, (1, c)) == late_tag, 1.0, 0.0)
                    eout[1, c, :BODY, :] = (total + body(ein, (1, c)) * keep).astype(BF)
                    eout[1, c, BODY:, :] = jnp.broadcast_to(late_tag, (PAD, HEAD)).astype(BF)
                    carry_copy(1, c).start()
                if at_z < last:
                    share_copy(c).start()

            @pl.loop(0, chunks)
            def _(c):
                @pl.when(c % 2 != x)
                def _():
                    swap_copy(1, c).wait_recv()
                    if at_z < last:
                        share_copy(c).wait_recv()

                got_one = jnp.where(tag(ein, (1, c)) == final, 1.0, 0.0)
                total = near_part(1, c, final) + body(ein, (1, c)) * got_one
                state[1, chunk_at(c), :] = total.astype(BF)

    def pair_copy(p):
        return rc(pair.at[0, :, span(p)], pair.at[1, :, span(p)], psem, p, mate)

    def heads_loop(begin, stop, step):
        @pl.loop(begin, stop)
        def _(h):
            step(h, pl.ds(pl.multiple_of(h * HEAD, HEAD), HEAD))

    def inside(h, at):
        fq = feature(q_ref[:, at].astype(F32)).astype(BF)
        fq_ref[:, at] = fq
        weight = dot(fq, fk_ref[:, at], 1, 1).astype(BF) * mask_ref[...]
        weight_ref[h] = weight
        attn_ref[:, at] = dot(weight, v_ref[:, at], 1, 0)

    def local(c):
        heads_loop(c * HC, (c + 1) * HC, inside)

    def finish_head(h):
        at = pl.ds(pl.multiple_of(h * HEAD, HEAD), HEAD)
        outer = dot(fq_ref[:, at], state[0, at, :], 1, 0)
        attn = attn_ref[:, at] + jnp.where(col_ref[...] == first, outer, 0.0)
        inv = lax.rsqrt(jnp.mean(attn * attn, axis=-1, keepdims=True) + EPS)
        attn_ref[:, at] = attn
        pair[0, :, at] = (attn * inv * gain_ref[:, at]).astype(BF)

    def finish(c):
        for i in range(HC):
            finish_head(c * HC + i)
            if isinstance(c, int):
                pair_copy(i).start()
        if not isinstance(c, int):
            pair_copy(c + 1).start()

    def rest_of_states():
        @pl.loop(1, chunks - 1)
        def _(c):
            carry(c)
            finish(c)

        later.swap.start()
        carry(chunks - 1)
        finish(jnp.int32(chunks - 1))

    def turn(block):
        @pl.loop(0, 2)
        def _(i):
            k = block.k + 2 * i
            turned[k, 0] = whole[k, :, mine_at].T
            turned[k, 1] = theirs[k].T

    def swapped(block):
        block.swap.wait_recv()
        block.theirs_side.start()
        block.theirs_core.start()

    def mine_here(block):
        block.mine_side.wait_recv()
        block.mine_core.start()

    def rest_here(block):
        block.rest_side.wait_recv()
        block.rest_core.start()

    def theirs_here(block):
        block.theirs_side.wait_recv()
        block.far_core.start()

    def lead_ready():
        for block in (early, more):
            theirs_here(block)
        for block in (early, more):
            block.theirs_core.wait_recv()
            block.mine_core.wait_recv()
            block.far_core.wait_recv()
        core_two.wait_recv()
        turn(early)

    def product(at, dest):
        k = jnp.int32(0)
        for b in range(2):
            k = k + (1 << b) * ((dest // (1 << b) + j // (1 << b)) % 2)
        value = dot(turned[k, 0], pair[0, :, at], 1, 0) + dot(turned[k, 1], pair[1, :, at], 1, 0)
        return value * factor

    def partial(p, dest):
        return product(span(p), dest)

    low = 1 - z // (depth // 2)

    def going(w, t):
        return z + (1 - 2 * w) * (last - t)

    def chain(w, p, dest, slot):
        return pltpu.make_async_remote_copy(
            src_ref=sent.at[dest, :, span(p)], dst_ref=got.at[slot, :, span(p)],
            send_sem=ssem.at[p * depth + dest], recv_sem=rsem.at[p * (depth + 1) + slot],
            device_id={"seq": lax.rem(me + 2 - 4 * w + n, n)}, device_id_type=MESH,
        )

    def slot_of(w, t):
        return going(w, t) * (1 - w) + depth * w if t == last - 1 else going(w, t)

    def on_way(w, t):
        return (z <= t) if w == 0 else (z >= last - t)

    def send_end(p, t):
        @pl.when(end)
        def _():
            w = 1 - low
            dest = going(w, t)
            sent[dest, :, span(p)] = partial(p, dest).astype(BF)
            chain(w, p, dest, slot_of(w, t)).start()

    def relay(p, w, t):
        @pl.when(inner)
        def _():
            dest = going(w, t)
            size = span(p).size
            acc[:, :size] = partial(p, dest)
            chain(w, p, dest, dest).wait_recv()
            sent[dest, :, span(p)] = (acc[:, :size] + got[dest, :, span(p)].astype(F32)).astype(BF)
            chain(w, p, dest, slot_of(w, t)).start()

    def onward(p, t):
        relay(p, 1 - low, t)

    def returning(p):
        relay(p, low, last - 1)

    def later_pieces(step, begin):
        @pl.loop(begin, pieces)
        def _(p):
            step(p)

    def paired(p, cond):
        @pl.when(cond)
        def _():
            pair_copy(p).wait_recv()

    def upstream(c):
        at = slice(c * BODY, (c + 1) * BODY)
        total = None
        for k in range(tp):
            owner = jnp.int32(0)
            for b in range(2):
                owner = owner + (1 << b) * (((k >> b) + j // (1 << b)) % 2)
            start = pl.multiple_of(owner * width, width)
            term = dot(whole[k], w_ref[at, pl.ds(start, width)], 1, 1)
            total = term if total is None else total + term
        left, right = [], []
        for i in range(HC):
            cut = slice(c * BODY + i * HEAD, c * BODY + (i + 1) * HEAD)
            attn = attn_ref[:, cut]
            inv = lax.rsqrt(jnp.mean(attn * attn, axis=-1, keepdims=True) + EPS)
            scaled = total[:, i * HEAD : (i + 1) * HEAD] * gain_ref[:, cut]
            mean = jnp.mean(attn * scaled, axis=-1, keepdims=True)
            grad = (scaled * inv - attn * (inv * inv * inv) * mean).astype(BF)
            grad_ref[:, cut] = grad
            left.append(jnp.where(col_ref[...] == first, fq_ref[:, cut].astype(F32), 0.0).astype(BF))
            right.append(grad)
        put(1, c, left, right, first)

    def inside_back(h, at):
        g = grad_ref[:, at]
        gw = dot(g, v_ref[:, at], 1, 1).astype(BF) * mask_ref[...]
        vp_ref[:, at] = dot(weight_ref[h], g, 0, 0)
        kp_ref[:, at] = dot(gw, fq_ref[:, at], 0, 0)
        outer = dot(g, state[0, at, :], 1, 1)
        qp = dot(gw, fk_ref[:, at], 1, 0) + jnp.where(col_ref[...] == first, outer, 0.0)
        oq_ref[:, at] = (qp * slope(q_ref[:, at].astype(F32))).astype(BF)

    def outside_back(h, at):
        late = col_ref[...] == final
        d = state[1, at, :]
        vp = vp_ref[:, at] + jnp.where(late, dot(fk_ref[:, at], d, 1, 0), 0.0)
        ov_ref[:, at] = vp.astype(BF)
        kp = kp_ref[:, at] + jnp.where(late, dot(v_ref[:, at], d, 1, 1), 0.0)
        ok_ref[:, at] = (kp * slope(k_ref[:, at].astype(F32))).astype(BF)

    def keys_put(c):
        ats = [slice((c * HC + i) * HEAD, (c * HC + i + 1) * HEAD) for i in range(HC)]
        picked = []
        for at in ats:
            fk = feature(k_ref[:, at].astype(F32))
            fk_ref[:, at] = fk.astype(BF)
            picked.append(jnp.where(col_ref[...] == final, fk, 0.0).astype(BF))
        put(0, c, picked, [v_ref[:, at] for at in ats], final)

    core_one.start()
    core_two.start()
    load_k.wait()
    load_v.wait()
    keys_put(0)

    @pl.when(lead == 0)
    def _():
        core_one.wait_recv()

    for block in (early, more):
        block.mine_side.start()
        block.swap.start()
    for c in range(1, chunks):
        keys_put(c)
    load_q.wait()
    load_w.start()
    local(0)
    carry_at(0, 0)
    local(1)
    carry_at(1, 0)
    local(2)
    swapped(early)
    carry_at(2, 0)
    local(3)
    mine_here(early)
    mine_here(more)
    swapped(more)

    @pl.when(lead == 1)
    def _():
        core_one.wait_recv()

    later.mine_side.start()
    for block in (early, more, later):
        block.rest_side.start()
    carry_at(3, 0)

    @pl.when(z < last)
    def _():
        rest_of_states()

    lead_ready()
    paired(0, end)
    send_end(0, 0)
    paired(1, end)
    send_end(1, 0)

    @pl.when(z == last)
    def _():
        rest_of_states()

    send_end(0, 2)
    send_end(1, 2)
    mine_here(later)
    paired(0, inner)
    onward(0, 1)
    paired(1, inner)
    onward(1, 1)
    paired(2, end)
    send_end(2, 0)
    send_end(2, 2)
    paired(3, end)
    send_end(3, 0)
    load_w.wait()
    for block in (early, more, later):
        rest_here(block)
    for block in (early, more, later):
        block.rest_core.wait_recv()
    later.mine_core.wait_recv()
    upstream(0)
    paired(2, inner)
    onward(2, 1)
    swapped(later)
    upstream(1)
    paired(4, end)
    send_end(4, 0)
    paired(3, inner)
    onward(3, 1)
    theirs_here(later)
    later.theirs_core.wait_recv()
    later.far_core.wait_recv()
    turn(later)
    send_end(0, 1)
    send_end(1, 1)
    send_end(2, 1)
    upstream(2)
    paired(4, inner)
    onward(4, 1)
    upstream(3)
    back(last)
    later_pieces(lambda p: send_end(p, 1), 3)
    send_end(3, 2)
    send_end(4, 2)
    onward(0, 2)
    onward(1, 2)
    returning(0)
    returning(1)
    returning(2)
    heads_loop(0, HC, inside_back)
    returning(3)
    onward(2, 2)
    heads_loop(HC, 2 * HC, inside_back)
    back(last - 1)
    onward(3, 2)
    back(last - 2)
    returning(4)
    heads_loop(2 * HC, 3 * HC, inside_back)
    onward(4, 2)
    heads_loop(3 * HC, 4 * HC, inside_back)

    @pl.loop(0, chunks)
    def _(c):
        at = chunk_at(c)
        ow_ref[:, at] = product(at, z)

    back(0)
    heads_loop(0, chunks * HC, outside_back)
    for p in range(pieces):
        for w in range(2):

            @pl.when((z > 0) if w == 0 else (z < last))
            def _():
                slot = z if w == 0 else depth
                chain(w, p, z, slot).wait_recv()
                ow_ref[:, span(p)] += got[slot, :, span(p)].astype(F32)

    for copy in [core_one, core_two] + early.all + more.all + later.all:
        copy.wait_send()
    for c in range(chunks):
        swap_copy(0, c).wait_send()
        swap_copy(1, c).wait_send()

        @pl.when(z < last)
        def _():
            carry_copy(0, c).wait_send()

        @pl.when((z > 0) & (x == c % 2))
        def _():
            carry_copy(1, c).wait_send()

        @pl.when((z < last) & (x == c % 2))
        def _():
            share_copy(c).wait_send()

    for p in range(pieces):
        pair_copy(p).wait_send()
        for w in range(2):
            for t in range(last):

                @pl.when(on_way(w, t))
                def _():
                    chain(w, p, going(w, t), slot_of(w, t)).wait_send()


def store_kernel(*refs):
    count = (len(refs) - 1) // 2
    sems = refs[-1]
    copies = []
    for i in range(count):
        rows = refs[i].shape[0] // 2
        for r in range(2):
            at = pl.ds(r * rows, rows)
            copies.append(pltpu.make_async_copy(refs[i].at[at], refs[count + i].at[at], sems.at[i, r]))
    for copy in copies:
        copy.start()
    for copy in copies:
        copy.wait()


def local_kernel(queries, keys, values, grad_out, out_weight, norm_gain, doc_ids):
    rows, feats = queries.shape
    n = lax.axis_size("seq")
    tp = lax.axis_size("tp")
    depth = n // 2
    model = out_weight.shape[1]
    width = model // tp
    mrows = model // n
    chunks = feats // BODY
    heads = feats // HEAD
    dims = (n, tp, depth, mrows, width, 1.0 / math.sqrt(rows * n))
    vmem = pl.BlockSpec(memory_space=pltpu.VMEM)
    anyspace = pl.BlockSpec(memory_space=pl.ANY)
    wide = jax.ShapeDtypeStruct((rows, feats), BF)
    summed = pltpu.VMEM((2, chunks, BODY + PAD, HEAD), BF)
    sem = pltpu.SemaphoreType.DMA
    flops = 2 * rows * model * feats * 3
    parts = pl.pallas_call(
        functools.partial(layer_kernel, dims),
        in_specs=[anyspace] * 5 + [vmem] * 2,
        out_specs=[vmem] * 4,
        out_shape=[pltpu.VMEM((rows, feats), BF)] * 3 + [pltpu.VMEM((mrows, feats), F32)],
        scratch_shapes=[
            pltpu.VMEM((rows, feats), BF),
            pltpu.VMEM((rows, feats), BF),
            pltpu.VMEM((rows, feats), BF),
            pltpu.VMEM((tp, rows, width), BF),
            pltpu.VMEM((tp, rows, mrows), BF),
            pltpu.VMEM((tp, 2, mrows, rows), BF),
            pltpu.VMEM((feats, model), BF),
            pltpu.VMEM((rows, feats), F32),
            pltpu.VMEM((rows, feats), BF),
            pltpu.VMEM((rows, feats), BF),
            pltpu.VMEM((heads, rows, rows), BF),
            pltpu.VMEM((rows, rows), BF),
            pltpu.VMEM((rows, HEAD), F32),
            pltpu.VMEM((2, rows, feats), BF),
            pltpu.VMEM((rows, feats), BF),
            pltpu.VMEM((rows, feats), F32),
            pltpu.VMEM((rows, feats), F32),
            pltpu.VMEM((2, feats, HEAD), BF),
            summed, summed, summed, summed,
            pltpu.VMEM((mrows, BODY), F32),
            pltpu.VMEM((depth, mrows, feats), BF),
            pltpu.VMEM((depth + 1, mrows, feats), BF),
            sem((5,)),
            sem((2, 26)),
            sem((2, chunks + 1)),
            sem((2, 2 * chunks)),
            sem((2, 2 * chunks)),
            sem((2, chunks)),
            sem(((chunks + 1) * depth,)),
            sem(((chunks + 1) * (depth + 1),)),
        ],
        compiler_params=pltpu.CompilerParams(
            collective_id=0, has_side_effects=True, vmem_limit_bytes=52 * 1024 * 1024
        ),
        cost_estimate=pl.CostEstimate(flops=flops, bytes_accessed=flops // 512, transcendentals=0),
        name="layer",
    )(queries, keys, values, grad_out, out_weight, norm_gain[None, :], doc_ids[None, :])
    return pl.pallas_call(
        store_kernel,
        in_specs=[vmem] * 4,
        out_specs=[anyspace] * 4,
        out_shape=[wide] * 3 + [jax.ShapeDtypeStruct((mrows, feats), F32)],
        scratch_shapes=[sem((4, 4))],
        compiler_params=pltpu.CompilerParams(vmem_limit_bytes=1024 * 1024),
        name="store",
    )(*parts)


def local_general(queries, keys, values, grad_out, out_weight, norm_gain, doc_ids):
    rows, feats = queries.shape
    n = lax.axis_size("seq")
    me = lax.axis_index("seq")
    heads = feats // HEAD

    def split(array):
        return array.reshape(rows, heads, HEAD)

    def mul(spec, a, b):
        return jnp.einsum(spec, a, b, preferred_element_type=F32)

    q, k = split(queries.astype(F32)), split(keys.astype(F32))
    v, gain = split(values), norm_gain.reshape(heads, HEAD)
    fq, fk = feature(q).astype(BF), feature(k).astype(BF)
    first, final = doc_ids[0], doc_ids[-1]
    early, late = (doc_ids == first)[:, None, None], (doc_ids == final)[:, None, None]
    firsts, finals = lax.all_gather(first, "seq"), lax.all_gather(final, "seq")
    before = (jnp.arange(n) < me) & (finals == first)
    after = (jnp.arange(n) > me) & (firsts == final)

    def over(summary, chosen):
        whole = lax.all_gather(summary, "seq")
        return jnp.sum(jnp.where(chosen[:, None, None, None], whole, 0.0), axis=0).astype(BF)

    at = jnp.arange(rows)
    mask = (at[:, None] >= at[None, :]) & (doc_ids[:, None] == doc_ids[None, :])
    weight = jnp.where(mask, mul("thd,shd->hts", fq, fk), 0.0).astype(BF)
    state = over(mul("shd,she->hde", jnp.where(late, fk, 0), v), before)
    attn = mul("hts,she->the", weight, v)
    attn = attn + jnp.where(early, mul("thd,hde->the", fq, state), 0.0)
    inv = lax.rsqrt(jnp.mean(attn * attn, axis=-1, keepdims=True) + EPS)
    normed = (attn * inv * gain).astype(BF).reshape(rows, feats)
    go = lax.all_gather(grad_out, "tp", axis=1, tiled=True)
    share = mul("tm,tf->mf", go, normed) * (1.0 / math.sqrt(rows * n))
    proj = lax.psum_scatter(share, "seq", scatter_dimension=0, tiled=True)
    scaled = split(mul("tm,fm->tf", go, out_weight)) * gain
    mean = jnp.mean(attn * scaled, axis=-1, keepdims=True)
    grad = (scaled * inv - attn * inv**3 * mean).astype(BF)
    dstate = over(mul("thd,the->hde", jnp.where(early, fq, 0), grad), after)
    gw = jnp.where(mask, mul("the,she->hts", grad, v), 0.0).astype(BF)
    vp = mul("hts,the->she", weight, grad) + jnp.where(late, mul("shd,hde->she", fk, dstate), 0.0)
    kp = mul("hts,thd->shd", gw, fq) + jnp.where(late, mul("she,hde->shd", v, dstate), 0.0)
    qp = mul("hts,shd->thd", gw, fk) + jnp.where(early, mul("the,hde->thd", grad, state), 0.0)
    outs = [qp * slope(q), kp * slope(k), vp]
    return tuple(o.astype(BF).reshape(rows, feats) for o in outs) + (proj,)


def solution(mesh):
    wide = P("seq", "tp")
    in_specs = (wide, wide, wide, wide, P("tp", None), P("tp"), P("seq"))
    local = local_kernel if mesh.shape["seq"] == 8 and mesh.shape["tp"] == 4 else local_general
    return jax.shard_map(
        local, mesh=mesh, in_specs=in_specs, out_specs=(wide,) * 4, check_vma=False
    )
```
